128 devices in a mesh: row: 8 (over y, core), col: 16 (over x, z).
Axes of the slice: x: 4, y: 4, z: 4, core: 2. Of those that a mesh axis runs over, the one named last changes fastest.
Arguments:
- ancestor: bfloat16 [128, 128, 256, 256], P('row', 'col'), may hold values from -6 to 6
- tile_mask: int32 [128, 128], P('row', 'col'), may hold values 0 or 1
- member_one: int32 [128], replicated, may hold values 0 or 1
- member_two: int32 [128], replicated, may hold values 0 or 1
- factor_one: bfloat16 [128, 256, 256], P('row'), may hold values from -0.03125 to 0.03125
- factor_two: bfloat16 [128, 256, 256], P('row'), may hold values from -0.03125 to 0.03125
- link_block: bfloat16 [256, 256], replicated, may hold values from -0.375 to 0.375
- inverse_one: float32 [256, 256], replicated, may hold values from -6 to 6
- inverse_two: float32 [256, 256], replicated, may hold values from -6 to 6
Outputs:
- column_one: bfloat16 [128, 256, 256], P(('row', 'col'))
- column_two: bfloat16 [128, 256, 256], P(('row', 'col'))
- diag_one: bfloat16 [256, 256], replicated
- cross_block: bfloat16 [256, 256], replicated
- diag_two: bfloat16 [256, 256], replicated
The draws below stay inside these ranges and needn't reach their ends.
All inputs are finite; a program needn't handle non-finite values. No bound on the sum of `tile_mask` on one device may be relied on, other than what follows from the above.
Results may differ from the reference program's by a relative error of at most 0.01.
Values may be sent and summed in bfloat16 or wider, within the bound.
A program may use at most 128 MiB of HBM per device.

```python
import jax
import jax.numpy as jnp
from jax import lax

TILE = 256
TILES = 128


def set_ends(drawn, stream_key, low, high):
    place = [jax.random.randint(jax.random.fold_in(stream_key, axis), (), 0, length) for axis, length in enumerate(drawn.shape)]
    widest = drawn.shape.index(max(drawn.shape))
    beside = place[:widest] + [(place[widest] + 1) % drawn.shape[widest]] + place[widest + 1:]
    return drawn.at[tuple(place)].set(low).at[tuple(beside)].set(high)


def levels(stream_key, shape, shards, least, largest):
    loudness, own = 1.0, jax.random.fold_in(stream_key, 6)
    for axis_at, parts in shards:
        steps = jnp.exp(jax.random.uniform(jax.random.fold_in(own, axis_at), (parts,), jnp.float32, least / len(shards), largest / len(shards)))
        loudness = loudness * jnp.repeat(steps, shape[axis_at] // parts).reshape([-1 if axis == axis_at else 1 for axis in range(len(shape))])
    return loudness


def normal_values(key, dims, deviation, most, shards=(), kind=jnp.bfloat16):
    array = deviation * jax.random.normal(key, dims, jnp.float32)
    if shards:
        array = array * levels(key, dims, shards, -0.22, 0.18)
    return jnp.clip(array, -most, most).astype(kind)


def setup_inputs(seed: int = 0) -> dict:
    streams_of = jax.random.split(jax.random.key(seed), 10)
    ancestor = normal_values(streams_of[0], (TILES, TILES, TILE, TILE), 1.0, 6.0, ((0, 8), (1, 16)))
    tile_mask = set_ends((jax.random.randint(streams_of[1], (TILES, TILES), 0, 5) < 3).astype(jnp.int32), jax.random.fold_in(streams_of[1], 1), 0, 1)
    member_one = set_ends((jax.random.randint(streams_of[2], (TILES,), 0, 4) < 3).astype(jnp.int32), jax.random.fold_in(streams_of[2], 1), 0, 1)
    member_two = set_ends((jax.random.randint(streams_of[3], (TILES,), 0, 4) < 3).astype(jnp.int32), jax.random.fold_in(streams_of[3], 1), 0, 1)
    factor_one = normal_values(streams_of[4], (TILES, TILE, TILE), (TILES * TILE) ** -0.5, 0.03125, ((0, 8),))
    factor_two = normal_values(streams_of[5], (TILES, TILE, TILE), (TILES * TILE) ** -0.5, 0.03125, ((0, 8),))
    link_block = normal_values(streams_of[6], (TILE, TILE), TILE ** -0.5, 0.375)
    inverse_one = normal_values(streams_of[7], (TILE, TILE), 1.0, 6.0, (), jnp.float32)
    inverse_two = normal_values(streams_of[8], (TILE, TILE), 1.0, 6.0, (), jnp.float32)
    return {"ancestor": ancestor, "tile_mask": tile_mask, "member_one": member_one, "member_two": member_two, "factor_one": factor_one, "factor_two": factor_two, "link_block": link_block, "inverse_one": inverse_one, "inverse_two": inverse_two}


def reference(ancestor, tile_mask, member_one, member_two, factor_one, factor_two, link_block, inverse_one, inverse_two):
    hp = lax.Precision.HIGHEST
    zero = jnp.zeros((), jnp.bfloat16)
    first = jnp.where(member_one[:, None, None] > 0, factor_one, zero)
    second = jnp.where(member_two[:, None, None] > 0, factor_two, zero)
    stacked = jnp.stack([first, second], 1).astype(jnp.float32)

    def one_row(item):
        tiles, marks = item
        kept = jnp.where(marks[:, None, None] > 0, tiles, zero).astype(jnp.float32)
        return jnp.einsum('jab,jkbc->kac', kept, stacked, precision=hp)

    products = lax.map(one_row, (ancestor, tile_mask))
    weight_one = member_one.astype(jnp.float32)[:, None, None]
    weight_two = member_two.astype(jnp.float32)[:, None, None]
    first_f = first.astype(jnp.float32)
    second_f = second.astype(jnp.float32)
    link_f = link_block.astype(jnp.float32)
    y_one = weight_one * products[:, 0]
    column_one = (-y_one).astype(jnp.bfloat16)
    diag_one = (inverse_one + jnp.einsum('sab,sac->bc', first_f, y_one, precision=hp)).astype(jnp.bfloat16)
    y_two = weight_two * (products[:, 1] + jnp.einsum('sab,bc->sac', column_one.astype(jnp.float32), link_f, precision=hp))
    column_two = (-y_two).astype(jnp.bfloat16)
    vsum = jnp.einsum('sab,sac->bc', column_one.astype(jnp.float32), second_f, precision=hp)
    cross_block = (-(vsum + jnp.dot(diag_one, link_block, preferred_element_type=jnp.float32))).astype(jnp.bfloat16)
    diag_two = inverse_two + jnp.einsum('sab,sac->bc', second_f, y_two, precision=hp)
    diag_two = (diag_two - jnp.dot(link_block.T, cross_block, preferred_element_type=jnp.float32)).astype(jnp.bfloat16)
    return column_one, column_two, diag_one, cross_block, diag_two
```

```python
import jax
import jax.numpy as jnp
from jax import lax
from jax.experimental import pallas as pl
from jax.experimental.pallas import tpu as pltpu
from jax.sharding import PartitionSpec as P

MESH = pl.DeviceIdType.MESH
F32 = jnp.float32
BF16 = jnp.bfloat16
ORDER = (
    (2, 2), (2, 1), (1, 2), (2, 0), (0, 2), (2, 3), (3, 2), (1, 3),
    (3, 1), (1, 0), (0, 1), (1, 1), (3, 3), (3, 0), (0, 3), (0, 0),
)
PAIR, RING_Y, RING_X, RING_Z, BACK_X, BACK_Y, BACK_PAIR = range(7)


def pick(index, values):
    out = jnp.int32(values[0])
    for k in range(1, len(values)):
        out = jnp.where(index == k, jnp.int32(values[k]), out)
    return out


def kernel(
    anc, tm, m1, m2, f1, f2, link, inv1, inv2,
    o1, o2, od1, oc, od2,
    A, L, Fl, Pb, B1, B2, C1, C2, R, Gf, Gs, Gr1, Hb, Gr2, Ib, Gr3, Jb, Fin, lk, i1, i2,
    semA, semF, semLr, semLy, semLp, ssem, rsem, gsend, grecv,
):
    T = anc.shape[2]
    half, quarter, sub = T // 2, T // 4, T // 32
    r = lax.axis_index("row")
    c = lax.axis_index("col")
    y, core = r // 2, r % 2
    x, z = c // 4, c % 4

    def at(dx=0, dy=0, dz=0, other_core=None):
        which = core if other_core is None else other_core
        return {"row": ((y + dy) % 4) * 2 + which, "col": ((x + dx) % 4) * 4 + (z + dz) % 4}

    members = (m1, m2)

    d = (y + 4 - x) % 4
    is_src = jnp.logical_and(d == 0, core == z // 2)
    off = 8 * (z % 2)

    def local_tile(p, j):
        return pltpu.make_async_copy((f1, f2)[p].at[off + j], L.at[p, j], semLr.at[p, j])

    @pl.when(is_src)
    def _():
        for p in range(2):
            for t in range(8):
                local_tile(p, (t % 2) * 4 + t // 2).start()

    def load_row(s):
        return pltpu.make_async_copy(anc.at[s], A.at[s], semA.at[s])

    for dx, dz in ORDER:
        load_row(((x + dx) % 4) * 4 + (z + dz) % 4).start()
    small = [
        pltpu.make_async_copy(f1, Fl.at[0], semF.at[0]),
        pltpu.make_async_copy(f2, Fl.at[1], semF.at[1]),
        pltpu.make_async_copy(link, lk, semF.at[2]),
        pltpu.make_async_copy(inv1, i1, semF.at[3]),
        pltpu.make_async_copy(inv2, i2, semF.at[4]),
    ]
    for copy in small:
        copy.start()

    barrier = pltpu.get_barrier_semaphore()
    partners = [at(other_core=1 - core)]
    for o in range(1, 4):
        partners += [at(dx=o), at(dz=o), at(dy=o), at(dy=o, other_core=1 - core)]
    for partner in partners:
        pl.semaphore_signal(barrier, inc=1, device_id=partner, device_id_type=MESH)
    pl.semaphore_wait(barrier, len(partners))

    def forward_parts(p, j):
        up = j < 4
        dd = jnp.where(up, d, (4 - d) % 4)
        hub = jnp.where(up, 0, 1)
        along = pltpu.make_async_remote_copy(
            src_ref=L.at[p, j], dst_ref=L.at[p, j], send_sem=semLy.at[p, j], recv_sem=semLr.at[p, j],
            device_id=at(dy=jnp.where(up, 1, 3), other_core=hub), device_id_type=MESH,
        )
        across = pltpu.make_async_remote_copy(
            src_ref=L.at[p, j], dst_ref=L.at[p, j], send_sem=semLp.at[p, j], recv_sem=semLr.at[p, j],
            device_id=at(other_core=1 - core), device_id_type=MESH,
        )
        relay = jnp.logical_and(d != 0, core == hub)
        do_along = jnp.logical_or(is_src, jnp.logical_and(relay, dd < 3))
        do_across = jnp.logical_or(is_src, relay)
        return along, across, do_along, do_across

    def forward(p, j):
        along, across, do_along, do_across = forward_parts(p, j)

        @pl.when(is_src)
        def _():
            local_tile(p, j).wait()

        @pl.when(jnp.logical_not(is_src))
        def _():
            across.wait_recv()

        @pl.when(do_along)
        def _():
            along.start()

        @pl.when(do_across)
        def _():
            across.start()

    def forward_end(p, j):
        along, across, do_along, do_across = forward_parts(p, j)

        @pl.when(do_along)
        def _():
            along.wait_send()

        @pl.when(do_across)
        def _():
            across.wait_send()

    def slot(h, du, dv):
        dx, dz = (du, dv) if h == 0 else (dv, du)
        return ((x + dx) % 4) * 4 + (z + dz) % 4

    def rs_copy(p, h, way, m, src, dst, stage):
        step = 1 if way == 0 else 3
        device = at(dx=step) if (h == 0) == (stage == 1) else at(dz=step)
        return pltpu.make_async_remote_copy(
            src_ref=src, dst_ref=dst, send_sem=ssem.at[p, h, way, m], recv_sem=rsem.at[p, h, way, m],
            device_id=device, device_id_type=MESH,
        )

    def rows_of(h):
        return pl.ds(h * half, half)

    def first_hop(p, h, way, k, src=None):
        return rs_copy(p, h, way, k, B1.at[p, h, way, k] if src is None else src, B1.at[p, h, way, k], 1)

    def second_hop(p, h, way, dv, src=None):
        return rs_copy(p, h, way, 2 + dv, B2.at[p, h, way, dv] if src is None else src, B2.at[p, h, way, dv], 1)

    def third_hop(p, h, way):
        src = B2.at[p, h, 0, 2, pl.ds(way * quarter, quarter)]
        return rs_copy(p, h, way, 6, src, C1.at[p, h, way], 2)

    def fourth_hop(p, h, way):
        return rs_copy(p, h, way, 7, B2.at[p, h, 0, 1 if way == 0 else 3], C2.at[p, h, way], 2)

    def product(p, i):
        dx, dz = pick(i, [v[0] for v in ORDER]), pick(i, [v[1] for v in ORDER])
        s = ((x + dx) % 4) * 4 + (z + dz) % 4
        if p == 0:
            load_row(s).wait()
        own = members[p][16 * r + s]
        acc = None
        for j in range(8):
            w = (tm[s, j] * own * members[p][8 * c + j]).astype(F32)
            a = A[s, j] * jnp.full((T, T), w, F32).astype(BF16)
            term = jnp.dot(a, L[p, j], preferred_element_type=F32)
            acc = term if acc is None else acc + term
        Pb[p, s] = acc.astype(BF16)
        for h in range(2):
            du, dv = (dx, dz) if h == 0 else (dz, dx)
            inner = jnp.logical_or(dv == 1, dv == 2)
            outer = jnp.logical_not(inner)
            src = Pb.at[p, s, rows_of(h)]

            @pl.when(jnp.logical_and(du == 2, inner))
            def _():
                first_hop(p, h, 0, dv - 1, src).start()

            @pl.when(jnp.logical_and(du == 2, outer))
            def _():
                first_hop(p, h, 1, dv // 3, src).start()

            @pl.when(jnp.logical_and(du == 1, outer))
            def _():
                second_hop(p, h, 0, dv, src).start()

            @pl.when(jnp.logical_and(du == 3, inner))
            def _():
                second_hop(p, h, 1, dv, src).start()

    def add_and_pass(p):
        for k in range(2):
            for h in range(2):
                for way in range(2):
                    du, dv = (1, k + 1) if way == 0 else (3, 3 * k)
                    first_hop(p, h, way, k).wait_recv()
                    mine = Pb[p, slot(h, du, dv), rows_of(h)].astype(F32)
                    B1[p, h, way, k] = (mine + B1[p, h, way, k].astype(F32)).astype(BF16)
                    second_hop(p, h, way, dv, B1.at[p, h, way, k]).start()

    def line_sum(p, h, dv):
        for way in range(2):
            second_hop(p, h, way, dv).wait_recv()
        total = Pb[p, slot(h, 0, dv), rows_of(h)].astype(F32)
        return total + B2[p, h, 0, dv].astype(F32) + B2[p, h, 1, dv].astype(F32)

    def stage_two_far(p):
        for h in range(2):
            B2[p, h, 0, 2] = line_sum(p, h, 2).astype(BF16)
            for way in range(2):
                third_hop(p, h, way).start()

    def stage_two_near(p):
        for h in range(2):
            for way, dv in ((0, 1), (1, 3)):
                B2[p, h, 0, dv] = line_sum(p, h, dv).astype(BF16)
        for h in range(2):
            for way, dv in ((0, 1), (1, 3)):
                third_hop(p, h, way).wait_recv()
                part = pl.ds(way * quarter, quarter)
                moved = B2[p, h, 0, dv, part].astype(F32) + C1[p, h, way].astype(F32)
                B2[p, h, 0, dv, part] = moved.astype(BF16)
                fourth_hop(p, h, way).start()
        for h in range(2):
            R[p, rows_of(h)] = line_sum(p, h, 0)

    def stage_two_end(p):
        for h in range(2):
            for way in range(2):
                fourth_hop(p, h, way).wait_recv()
            R[p, rows_of(h)] = R[p, rows_of(h)] + C2[p, h, 0].astype(F32) + C2[p, h, 1].astype(F32)

    for t in range(8):
        forward(0, (t % 2) * 4 + t // 2)

    @pl.loop(0, 16)
    def _(i):
        product(0, i)

        @pl.when(i % 2 == 1)
        def _():
            t = i // 2
            forward(1, (t % 2) * 4 + t // 2)

    add_and_pass(0)

    @pl.loop(0, 16)
    def _(i):
        product(1, i)

    for copy in small:
        copy.wait()
    Gf[...] = jnp.zeros_like(Gf)

    def contract(a, b):
        return lax.dot_general(a, b, (((0,), (0,)), ((), ())), preferred_element_type=F32)

    @pl.loop(0, 16)
    def _(s):
        two = jnp.full((T, T), m2[16 * r + s].astype(F32), F32).astype(BF16)
        pieces = (
            contract(Fl[0, s], Pb[0, s]),
            contract(Fl[1, s], Pb[0, s] * two),
            contract(Fl[1, s], Pb[1, s]),
        )
        for k in range(3):
            Gf[:, k] += pieces[k].reshape(32, sub, T)

    Gs[...] = Gf[...].astype(BF16)

    def g_copy(kind, o, src, dst, device):
        return pltpu.make_async_remote_copy(
            src_ref=src, dst_ref=dst, send_sem=gsend.at[kind, o], recv_sem=grecv.at[kind, o],
            device_id=device, device_id_type=MESH,
        )

    g = core * 16 + y * 4 + x
    g_pair = g_copy(PAIR, 0, Gs.at[pl.ds((1 - core) * 16, 16)], Gr1, at(other_core=1 - core))
    g_y = [
        g_copy(RING_Y, o - 1, Hb.at[pl.ds((y + o) % 4 * 4, 4)], Gr2.at[o - 1], at(dy=o)) for o in range(1, 4)
    ]
    g_x = [g_copy(RING_X, o - 1, Ib.at[(x + o) % 4], Gr3.at[o - 1], at(dx=o)) for o in range(1, 4)]
    g_z = [g_copy(RING_Z, o - 1, Jb.at[z], Jb.at[z], at(dz=o)) for o in range(1, 4)]
    b_x = [g_copy(BACK_X, o - 1, Fin.at[g], Fin.at[g], at(dx=o)) for o in range(1, 4)]
    b_y = []
    for o in range(1, 4):
        part = Fin.at[pl.ds(core * 16 + y * 4, 4)]
        b_y.append(g_copy(BACK_Y, o - 1, part, part, at(dy=o)))
    part = Fin.at[pl.ds(core * 16, 16)]
    b_pair = g_copy(BACK_PAIR, 0, part, part, at(other_core=1 - core))

    g_pair.start()
    stage_two_far(0)
    g_pair.wait_recv()
    Hb[...] = (Gf[pl.ds(core * 16, 16)] + Gr1[...].astype(F32)).astype(BF16)
    for copy in g_y:
        copy.start()
    add_and_pass(1)
    for copy in g_y:
        copy.wait_recv()
    total = Hb[pl.ds(y * 4, 4)].astype(F32)
    for o in range(3):
        total += Gr2[o].astype(F32)
    Ib[...] = total.astype(BF16)
    for copy in g_x:
        copy.start()
    stage_two_near(0)
    for copy in g_x:
        copy.wait_recv()
    total = Ib[x].astype(F32)
    for o in range(3):
        total += Gr3[o].astype(F32)
    Jb[z] = total.astype(BF16)
    for copy in g_z:
        copy.start()
    stage_two_end(0)
    stage_two_far(1)
    for copy in g_z:
        copy.wait_recv()
    total = Jb[0].astype(F32)
    for o in range(1, 4):
        total += Jb[o].astype(F32)
    rows = pl.ds(pl.multiple_of(g * sub, sub), sub)
    Fin[g, 0] = (i1[rows] + total[0]).astype(BF16)
    Fin[g, 1] = total[1].astype(BF16)
    Fin[g, 2] = (i2[rows] + total[2]).astype(BF16)
    for copy in b_x:
        copy.start()
    stage_two_near(1)
    for copy in b_x:
        copy.wait_recv()
    for copy in b_y:
        copy.start()
    col = (-R[0]).astype(BF16)
    o1[0] = col
    linked = jnp.dot(col, lk[...], preferred_element_type=F32)
    R[0] = linked * m2[16 * r + c].astype(F32)
    for copy in b_y:
        copy.wait_recv()
    b_pair.start()
    stage_two_end(1)
    o2[0] = (-(R[1] + R[0])).astype(BF16)
    b_pair.wait_recv()
    d1 = Fin[:, 0].astype(F32).reshape(T, T).astype(BF16)
    s21 = Fin[:, 1].astype(F32).reshape(T, T)
    od1[...] = d1
    cross = (s21.T - jnp.dot(d1, lk[...], preferred_element_type=F32)).astype(BF16)
    oc[...] = cross
    d2 = Fin[:, 2].astype(F32).reshape(T, T)
    d2 = d2 - jnp.dot(s21.astype(BF16), lk[...], preferred_element_type=F32)
    od2[...] = (d2 - contract(lk[...], cross)).astype(BF16)

    for p in range(2):
        for j in range(8):
            forward_end(p, j)
        for h in range(2):
            for way in range(2):
                for k in range(2):
                    first_hop(p, h, way, k).wait_send()
                for dv in range(4):
                    second_hop(p, h, way, dv).wait_send()
                third_hop(p, h, way).wait_send()
                fourth_hop(p, h, way).wait_send()
    for copy in [g_pair, *g_y, *g_x, *g_z, *b_x, *b_y, b_pair]:
        copy.wait_send()


def shards(anc, tm, m1, m2, f1, f2, link, inv1, inv2):
    T = anc.shape[2]
    half, quarter, sub = T // 2, T // 4, T // 32
    any_space = pl.BlockSpec(memory_space=pl.ANY)
    smem = pl.BlockSpec(memory_space=pltpu.SMEM)
    vmem = pl.BlockSpec(memory_space=pltpu.VMEM)
    dma = pltpu.SemaphoreType.DMA
    tile = jax.ShapeDtypeStruct((T, T), BF16)
    column = jax.ShapeDtypeStruct((1, T, T), BF16)
    return pl.pallas_call(
        kernel,
        out_shape=(column, column, tile, tile, tile),
        in_specs=[any_space, smem, smem, smem, any_space, any_space, any_space, any_space, any_space],
        out_specs=(vmem,) * 5,
        scratch_shapes=[
            pltpu.VMEM((16, 8, T, T), BF16),
            pltpu.VMEM((2, 8, T, T), BF16),
            pltpu.VMEM((2, 16, T, T), BF16),
            pltpu.VMEM((2, 16, T, T), BF16),
            pltpu.VMEM((2, 2, 2, 2, half, T), BF16),
            pltpu.VMEM((2, 2, 2, 4, half, T), BF16),
            pltpu.VMEM((2, 2, 2, quarter, T), BF16),
            pltpu.VMEM((2, 2, 2, half, T), BF16),
            pltpu.VMEM((2, T, T), F32),
            pltpu.VMEM((32, 3, sub, T), F32),
            pltpu.VMEM((32, 3, sub, T), BF16),
            pltpu.VMEM((16, 3, sub, T), BF16),
            pltpu.VMEM((16, 3, sub, T), BF16),
            pltpu.VMEM((3, 4, 3, sub, T), BF16),
            pltpu.VMEM((4, 3, sub, T), BF16),
            pltpu.VMEM((3, 3, sub, T), BF16),
            pltpu.VMEM((4, 3, sub, T), BF16),
            pltpu.VMEM((32, 3, sub, T), BF16),
            pltpu.VMEM((T, T), BF16),
            pltpu.VMEM((T, T), F32),
            pltpu.VMEM((T, T), F32),
            dma((16,)),
            dma((5,)),
            dma((2, 8)),
            dma((2, 8)),
            dma((2, 8)),
            dma((2, 2, 2, 8)),
            dma((2, 2, 2, 8)),
            dma((7, 3)),
            dma((7, 3)),
        ],
        compiler_params=pltpu.CompilerParams(
            collective_id=0, has_side_effects=True, vmem_limit_bytes=60 * 1024 * 1024
        ),
    )(anc, tm, m1, m2, f1, f2, link, inv1, inv2)


def solution(mesh):
    in_specs = (
        P("row", "col", None, None),
        P("row", "col"),
        P(),
        P(),
        P("row", None, None),
        P("row", None, None),
        P(),
        P(),
        P(),
    )
    out_specs = (P(("row", "col"), None, None), P(("row", "col"), None, None), P(), P(), P())
    return jax.shard_map(shards, mesh=mesh, in_specs=in_specs, out_specs=out_specs, check_vma=False)
```

```python
import jax
import jax.numpy as jnp
from jax import lax
from jax.experimental import pallas as pl
from jax.experimental.pallas import tpu as pltpu
from jax.sharding import PartitionSpec as P

MESH = pl.DeviceIdType.MESH
F32 = jnp.float32
BF16 = jnp.bfloat16
ORDER = (
    (2, 2), (2, 1), (1, 2), (2, 0), (0, 2), (2, 3), (3, 2), (1, 3),
    (3, 1), (1, 0), (0, 1), (1, 1), (3, 3), (3, 0), (0, 3), (0, 0),
)
PAIR, RING_Y, RING_X, RING_Z, BACK_X, BACK_Y, BACK_PAIR = range(7)


def pick(index, values):
    out = jnp.int32(values[0])
    for k in range(1, len(values)):
        out = jnp.where(index == k, jnp.int32(values[k]), out)
    return out


def kernel(
    anc, tm, m1, m2, f1, f2, link, inv1, inv2,
    o1, o2, od1, oc, od2,
    A, L, Fl, Pb, B1, B2, C1, C2, R, Gf, Gs, Gr1, Hb, Gr2, Ib, Gr3, Jb, Fin, lk, i1, i2,
    semA, semF, semLr, semLy, semLp, ssem, rsem, gsend, grecv,
):
    T = anc.shape[2]
    half, quarter, sub = T // 2, T // 4, T // 32
    r = lax.axis_index("row")
    c = lax.axis_index("col")
    y, core = r // 2, r % 2
    x, z = c // 4, c % 4

    def at(dx=0, dy=0, dz=0, other_core=None):
        which = core if other_core is None else other_core
        return {"row": ((y + dy) % 4) * 2 + which, "col": ((x + dx) % 4) * 4 + (z + dz) % 4}

    members = (m1, m2)

    d = (y + 4 - x) % 4
    is_src = jnp.logical_and(d == 0, core == z // 2)
    off = 8 * (z % 2)

    def local_tile(p, j):
        return pltpu.make_async_copy((f1, f2)[p].at[off + j], L.at[p, j], semLr.at[p, j])

    @pl.when(is_src)
    def _():
        for p in range(2):
            for t in range(8):
                local_tile(p, (t % 2) * 4 + t // 2).start()

    def load_row(s):
        return pltpu.make_async_copy(anc.at[s], A.at[s], semA.at[s])

    for dx, dz in ORDER:
        load_row(((x + dx) % 4) * 4 + (z + dz) % 4).start()
    small = [
        pltpu.make_async_copy(f1, Fl.at[0], semF.at[0]),
        pltpu.make_async_copy(f2, Fl.at[1], semF.at[1]),
        pltpu.make_async_copy(link, lk, semF.at[2]),
        pltpu.make_async_copy(inv1, i1, semF.at[3]),
        pltpu.make_async_copy(inv2, i2, semF.at[4]),
    ]
    for copy in small:
        copy.start()

    barrier = pltpu.get_barrier_semaphore()
    partners = [at(other_core=1 - core)]
    for o in range(1, 4):
        partners += [at(dx=o), at(dz=o), at(dy=o), at(dy=o, other_core=1 - core)]
    for partner in partners:
        pl.semaphore_signal(barrier, inc=1, device_id=partner, device_id_type=MESH)
    pl.semaphore_wait(barrier, len(partners))

    away = jnp.where(core == 0, d, (4 - d) % 4)
    inside = d != 0
    relays = jnp.logical_and(inside, away < 3)
    fed = jnp.logical_and(d == 0, jnp.logical_not(is_src))

    def along(p, j, up):
        return pltpu.make_async_remote_copy(
            src_ref=L.at[p, j], dst_ref=L.at[p, j], send_sem=semLy.at[p, j], recv_sem=semLr.at[p, j],
            device_id=at(dy=jnp.where(up, 1, 3), other_core=jnp.where(up, 0, 1)), device_id_type=MESH,
        )

    def across(p, j):
        return pltpu.make_async_remote_copy(
            src_ref=L.at[p, j], dst_ref=L.at[p, j], send_sem=semLp.at[p, j], recv_sem=semLr.at[p, j],
            device_id=at(other_core=1 - core), device_id_type=MESH,
        )

    def forward(p, k):
        mine = 4 * core + k

        @pl.when(is_src)
        def _():
            for up in (True, False):
                j = k if up else 4 + k
                local_tile(p, j).wait()
                along(p, j, up).start()
                across(p, j).start()

        @pl.when(inside)
        def _():
            across(p, mine).wait_recv()

        @pl.when(relays)
        def _():
            along(p, mine, core == 0).start()

        @pl.when(inside)
        def _():
            across(p, mine).start()

    def arrived(p):
        for k in range(4):

            @pl.when(jnp.logical_not(is_src))
            def _():
                across(p, 4 * (1 - core) + k).wait_recv()

            @pl.when(fed)
            def _():
                across(p, 4 * core + k).wait_recv()

    def forward_end(p, k):
        mine = 4 * core + k

        @pl.when(is_src)
        def _():
            for up in (True, False):
                j = k if up else 4 + k
                along(p, j, up).wait_send()
                across(p, j).wait_send()

        @pl.when(relays)
        def _():
            along(p, mine, core == 0).wait_send()

        @pl.when(inside)
        def _():
            across(p, mine).wait_send()

    def slot(h, du, dv):
        dx, dz = (du, dv) if h == 0 else (dv, du)
        return ((x + dx) % 4) * 4 + (z + dz) % 4

    def rs_copy(p, h, way, m, src, dst, stage):
        step = 1 if way == 0 else 3
        device = at(dx=step) if (h == 0) == (stage == 1) else at(dz=step)
        return pltpu.make_async_remote_copy(
            src_ref=src, dst_ref=dst, send_sem=ssem.at[p, h, way, m], recv_sem=rsem.at[p, h, way, m],
            device_id=device, device_id_type=MESH,
        )

    def rows_of(h):
        return pl.ds(h * half, half)

    def first_hop(p, h, way, k, src=None):
        return rs_copy(p, h, way, k, B1.at[p, h, way, k] if src is None else src, B1.at[p, h, way, k], 1)

    def second_hop(p, h, way, dv, src=None):
        return rs_copy(p, h, way, 2 + dv, B2.at[p, h, way, dv] if src is None else src, B2.at[p, h, way, dv], 1)

    def third_hop(p, h, way):
        src = B2.at[p, h, 0, 2, pl.ds(way * quarter, quarter)]
        return rs_copy(p, h, way, 6, src, C1.at[p, h, way], 2)

    def fourth_hop(p, h, way):
        return rs_copy(p, h, way, 7, B2.at[p, h, 0, 1 if way == 0 else 3], C2.at[p, h, way], 2)

    def product(p, i):
        dx, dz = pick(i, [v[0] for v in ORDER]), pick(i, [v[1] for v in ORDER])
        s = ((x + dx) % 4) * 4 + (z + dz) % 4
        if p == 0:
            load_row(s).wait()
        own = members[p][16 * r + s]
        acc = None
        for j in range(8):
            w = (tm[j, s] * own * members[p][8 * c + j]).astype(F32)
            a = A[s, j] * jnp.full((T, T), w, F32).astype(BF16)
            term = jnp.dot(a, L[p, j], preferred_element_type=F32)
            acc = term if acc is None else acc + term
        Pb[p, s] = acc.astype(BF16)
        for h in range(2):
            du, dv = (dx, dz) if h == 0 else (dz, dx)
            inner = jnp.logical_or(dv == 1, dv == 2)
            outer = jnp.logical_not(inner)
            src = Pb.at[p, s, rows_of(h)]

            @pl.when(jnp.logical_and(du == 2, inner))
            def _():
                first_hop(p, h, 0, dv - 1, src).start()

            @pl.when(jnp.logical_and(du == 2, outer))
            def _():
                first_hop(p, h, 1, dv // 3, src).start()

            @pl.when(jnp.logical_and(du == 1, outer))
            def _():
                second_hop(p, h, 0, dv, src).start()

            @pl.when(jnp.logical_and(du == 3, inner))
            def _():
                second_hop(p, h, 1, dv, src).start()

    def add_and_pass(p):
        for k in range(2):
            for h in range(2):
                for way in range(2):
                    du, dv = (1, k + 1) if way == 0 else (3, 3 * k)
                    first_hop(p, h, way, k).wait_recv()
                    mine = Pb[p, slot(h, du, dv), rows_of(h)].astype(F32)
                    B1[p, h, way, k] = (mine + B1[p, h, way, k].astype(F32)).astype(BF16)
                    second_hop(p, h, way, dv, B1.at[p, h, way, k]).start()

    def line_sum(p, h, dv):
        for way in range(2):
            second_hop(p, h, way, dv).wait_recv()
        total = Pb[p, slot(h, 0, dv), rows_of(h)].astype(F32)
        return total + B2[p, h, 0, dv].astype(F32) + B2[p, h, 1, dv].astype(F32)

    def stage_two_far(p):
        for h in range(2):
            B2[p, h, 0, 2] = line_sum(p, h, 2).astype(BF16)
            for way in range(2):
                third_hop(p, h, way).start()

    def stage_two_near(p):
        for h in range(2):
            for way, dv in ((0, 1), (1, 3)):
                B2[p, h, 0, dv] = line_sum(p, h, dv).astype(BF16)
        for h in range(2):
            for way, dv in ((0, 1), (1, 3)):
                third_hop(p, h, way).wait_recv()
                part = pl.ds(way * quarter, quarter)
                moved = B2[p, h, 0, dv, part].astype(F32) + C1[p, h, way].astype(F32)
                B2[p, h, 0, dv, part] = moved.astype(BF16)
                fourth_hop(p, h, way).start()
        for h in range(2):
            R[p, rows_of(h)] = line_sum(p, h, 0)

    def stage_two_end(p):
        for h in range(2):
            for way in range(2):
                fourth_hop(p, h, way).wait_recv()
            R[p, rows_of(h)] = R[p, rows_of(h)] + C2[p, h, 0].astype(F32) + C2[p, h, 1].astype(F32)

    for k in range(4):
        forward(0, k)
    arrived(0)

    @pl.loop(0, 16)
    def _(i):
        product(0, i)

        @pl.when(jnp.logical_and(i % 3 == 2, i < 12))
        def _():
            forward(1, i // 3)

    add_and_pass(0)
    arrived(1)

    @pl.loop(0, 16)
    def _(i):
        product(1, i)

    for copy in small:
        copy.wait()
    Gf[...] = jnp.zeros_like(Gf)

    def contract(a, b):
        return lax.dot_general(a, b, (((0,), (0,)), ((), ())), preferred_element_type=F32)

    @pl.loop(0, 16)
    def _(s):
        two = jnp.full((T, T), m2[16 * r + s].astype(F32), F32).astype(BF16)
        pieces = (
            contract(Fl[0, s], Pb[0, s]),
            contract(Fl[1, s], Pb[0, s] * two),
            contract(Fl[1, s], Pb[1, s]),
        )
        for k in range(3):
            Gf[:, k] += pieces[k].reshape(32, sub, T)

    Gs[...] = Gf[...].astype(BF16)

    def g_copy(kind, o, src, dst, device):
        return pltpu.make_async_remote_copy(
            src_ref=src, dst_ref=dst, send_sem=gsend.at[kind, o], recv_sem=grecv.at[kind, o],
            device_id=device, device_id_type=MESH,
        )

    g = core * 16 + y * 4 + x
    g_pair = g_copy(PAIR, 0, Gs.at[pl.ds((1 - core) * 16, 16)], Gr1, at(other_core=1 - core))
    g_y = [
        g_copy(RING_Y, o - 1, Hb.at[pl.ds((y + o) % 4 * 4, 4)], Gr2.at[o - 1], at(dy=o)) for o in range(1, 4)
    ]
    g_x = [g_copy(RING_X, o - 1, Ib.at[(x + o) % 4], Gr3.at[o - 1], at(dx=o)) for o in range(1, 4)]
    g_z = [g_copy(RING_Z, o - 1, Jb.at[z], Jb.at[z], at(dz=o)) for o in range(1, 4)]
    b_x = [g_copy(BACK_X, o - 1, Fin.at[g], Fin.at[g], at(dx=o)) for o in range(1, 4)]
    b_y = []
    for o in range(1, 4):
        part = Fin.at[pl.ds(core * 16 + y * 4, 4)]
        b_y.append(g_copy(BACK_Y, o - 1, part, part, at(dy=o)))
    part = Fin.at[pl.ds(core * 16, 16)]
    b_pair = g_copy(BACK_PAIR, 0, part, part, at(other_core=1 - core))

    g_pair.start()
    stage_two_far(0)
    g_pair.wait_recv()
    Hb[...] = (Gf[pl.ds(core * 16, 16)] + Gr1[...].astype(F32)).astype(BF16)
    for copy in g_y:
        copy.start()
    add_and_pass(1)
    for copy in g_y:
        copy.wait_recv()
    total = Hb[pl.ds(y * 4, 4)].astype(F32)
    for o in range(3):
        total += Gr2[o].astype(F32)
    Ib[...] = total.astype(BF16)
    for copy in g_x:
        copy.start()
    stage_two_near(0)
    for copy in g_x:
        copy.wait_recv()
    total = Ib[x].astype(F32)
    for o in range(3):
        total += Gr3[o].astype(F32)
    Jb[z] = total.astype(BF16)
    for copy in g_z:
        copy.start()
    stage_two_end(0)
    stage_two_far(1)
    for copy in g_z:
        copy.wait_recv()
    total = Jb[0].astype(F32)
    for o in range(1, 4):
        total += Jb[o].astype(F32)
    rows = pl.ds(pl.multiple_of(g * sub, sub), sub)
    Fin[g, 0] = (i1[rows] + total[0]).astype(BF16)
    Fin[g, 1] = total[1].astype(BF16)
    Fin[g, 2] = (i2[rows] + total[2]).astype(BF16)
    for copy in b_x:
        copy.start()
    stage_two_near(1)
    for copy in b_x:
        copy.wait_recv()
    for copy in b_y:
        copy.start()
    col = (-R[0]).astype(BF16)
    o1[0] = col
    linked = jnp.dot(col, lk[...], preferred_element_type=F32)
    R[0] = linked * m2[16 * r + c].astype(F32)
    for copy in b_y:
        copy.wait_recv()
    b_pair.start()
    stage_two_end(1)
    o2[0] = (-(R[1] + R[0])).astype(BF16)
    b_pair.wait_recv()
    d1 = Fin[:, 0].astype(F32).reshape(T, T).astype(BF16)
    s21 = Fin[:, 1].astype(F32).reshape(T, T)
    od1[...] = d1
    cross = (s21.T - jnp.dot(d1, lk[...], preferred_element_type=F32)).astype(BF16)
    oc[...] = cross
    d2 = Fin[:, 2].astype(F32).reshape(T, T)
    d2 = d2 - jnp.dot(s21.astype(BF16), lk[...], preferred_element_type=F32)
    od2[...] = (d2 - contract(lk[...], cross)).astype(BF16)

    for p in range(2):
        for k in range(4):
            forward_end(p, k)
        for h in range(2):
            for way in range(2):
                for k in range(2):
                    first_hop(p, h, way, k).wait_send()
                for dv in range(4):
                    second_hop(p, h, way, dv).wait_send()
                third_hop(p, h, way).wait_send()
                fourth_hop(p, h, way).wait_send()
    for copy in [g_pair, *g_y, *g_x, *g_z, *b_x, *b_y, b_pair]:
        copy.wait_send()


def hand_on(*refs):
    for k in range(5):
        refs[5 + k][...] = refs[k][...]


def shards(anc, tm, m1, m2, f1, f2, link, inv1, inv2):
    T = anc.shape[2]
    half, quarter, sub = T // 2, T // 4, T // 32
    any_space = pl.BlockSpec(memory_space=pl.ANY)
    smem = pl.BlockSpec(memory_space=pltpu.SMEM)
    vmem = pl.BlockSpec(memory_space=pltpu.VMEM)
    dma = pltpu.SemaphoreType.DMA
    tile = jax.ShapeDtypeStruct((T, T), BF16)
    column = jax.ShapeDtypeStruct((1, T, T), BF16)
    parts = pl.pallas_call(
        kernel,
        out_shape=(column, column, tile, tile, tile),
        in_specs=[any_space, smem, smem, smem, any_space, any_space, any_space, any_space, any_space],
        out_specs=(vmem,) * 5,
        scratch_shapes=[
            pltpu.VMEM((16, 8, T, T), BF16),
            pltpu.VMEM((2, 8, T, T), BF16),
            pltpu.VMEM((2, 16, T, T), BF16),
            pltpu.VMEM((2, 16, T, T), BF16),
            pltpu.VMEM((2, 2, 2, 2, half, T), BF16),
            pltpu.VMEM((2, 2, 2, 4, half, T), BF16),
            pltpu.VMEM((2, 2, 2, quarter, T), BF16),
            pltpu.VMEM((2, 2, 2, half, T), BF16),
            pltpu.VMEM((2, T, T), F32),
            pltpu.VMEM((32, 3, sub, T), F32),
            pltpu.VMEM((32, 3, sub, T), BF16),
            pltpu.VMEM((16, 3, sub, T), BF16),
            pltpu.VMEM((16, 3, sub, T), BF16),
            pltpu.VMEM((3, 4, 3, sub, T), BF16),
            pltpu.VMEM((4, 3, sub, T), BF16),
            pltpu.VMEM((3, 3, sub, T), BF16),
            pltpu.VMEM((4, 3, sub, T), BF16),
            pltpu.VMEM((32, 3, sub, T), BF16),
            pltpu.VMEM((T, T), BF16),
            pltpu.VMEM((T, T), F32),
            pltpu.VMEM((T, T), F32),
            dma((16,)),
            dma((5,)),
            dma((2, 8)),
            dma((2, 8)),
            dma((2, 8)),
            dma((2, 2, 2, 8)),
            dma((2, 2, 2, 8)),
            dma((7, 3)),
            dma((7, 3)),
        ],
        compiler_params=pltpu.CompilerParams(
            collective_id=0, has_side_effects=True, vmem_limit_bytes=60 * 1024 * 1024
        ),
    )(anc, tm.T, m1, m2, f1, f2, link, inv1, inv2)
    return pl.pallas_call(
        hand_on,
        out_shape=(column, column, tile, tile, tile),
        in_specs=[vmem] * 5,
        out_specs=(vmem,) * 5,
    )(*parts)


def solution(mesh):
    in_specs = (
        P("row", "col", None, None),
        P("row", "col"),
        P(),
        P(),
        P("row", None, None),
        P("row", None, None),
        P(),
        P(),
        P(),
    )
    out_specs = (P(("row", "col"), None, None), P(("row", "col"), None, None), P(), P(), P())
    return jax.shard_map(shards, mesh=mesh, in_specs=in_specs, out_specs=out_specs, check_vma=False)
```

```python
import jax
import jax.numpy as jnp
from jax import lax
from jax.experimental import pallas as pl
from jax.experimental.pallas import tpu as pltpu
from jax.sharding import PartitionSpec as P

MESH = pl.DeviceIdType.MESH
F32 = jnp.float32
BF16 = jnp.bfloat16
ORDER = (
    (2, 2), (2, 1), (1, 2), (2, 0), (0, 2), (2, 3), (3, 2), (1, 3),
    (3, 1), (1, 0), (0, 1), (1, 1), (3, 3), (3, 0), (0, 3), (0, 0),
)


def pick(index, values):
    out = jnp.int32(values[0])
    for k in range(1, len(values)):
        out = jnp.where(index == k, jnp.int32(values[k]), out)
    return out


def kernel(
    anc, tm, m1, m2, f1, f2, link, inv1, inv2,
    o1, o2, od1, oc, od2,
    O, semO, A, L, X, Fl, U, Pb, B1, B2, C, R, Gf, Gs, Gr1, Hb, Gr2, Jb, Fin, lk, i1, i2,
    semA, semF, semLr, semLy, semLp, semXr, semXs, semOs, ssem, rsem, gsend, grecv,
):
    T = anc.shape[2]
    half, sub = T // 2, T // 32
    r = lax.axis_index("row")
    c = lax.axis_index("col")
    y, core = r // 2, r % 2
    x, z = c // 4, c % 4

    def at(dx=0, dy=0, dz=0, other_core=None):
        which = core if other_core is None else other_core
        return {"row": ((y + dy) % 4) * 2 + which, "col": ((x + dx) % 4) * 4 + (z + dz) % 4}

    members = (m1, m2)

    d = (y + 4 - x) % 4
    own_core = core == z // 2
    off = 8 * (z % 2)
    is_src = jnp.logical_and(d == 0, own_core)
    fed = jnp.logical_and(d == 0, jnp.logical_not(own_core))
    inside = d != 0
    up_core = core == 0
    down_core = core == 1
    away = jnp.where(up_core, d, (4 - d) % 4)
    onward = (away == 1, jnp.logical_or(away == 1, away == 2))
    early = jnp.logical_or(away == 1, d == 0)

    def tile_of(k, up):
        return jnp.where(up, 0, 4) + k // 2

    def half_of(k):
        return pl.ds(k % 2 * half, half)

    def piece(p, k, up):
        return L.at[p, tile_of(k, up), half_of(k)]

    def stored(p, k, up):
        return (f1, f2)[p].at[off + tile_of(k, up), half_of(k)]

    def number(k, up):
        return jnp.where(up, 0, 8) + k

    def local_piece(p, k, up):
        return pltpu.make_async_copy(stored(p, k, up), piece(p, k, up), semLr.at[p, number(k, up)])

    def along(p, k, up, src):
        n = number(k, up)
        return pltpu.make_async_remote_copy(
            src_ref=src, dst_ref=piece(p, k, up), send_sem=semLy.at[p, n], recv_sem=semLr.at[p, n],
            device_id=at(dy=jnp.where(up, 1, 3), other_core=jnp.where(up, 0, 1)), device_id_type=MESH,
        )

    def across(p, k, up, src=None):
        n = number(k, up)
        return pltpu.make_async_remote_copy(
            src_ref=piece(p, k, up) if src is None else src, dst_ref=piece(p, k, up),
            send_sem=semLp.at[p, n], recv_sem=semLr.at[p, n],
            device_id=at(other_core=1 - core), device_id_type=MESH,
        )

    def detour_in(k, up):
        return pltpu.make_async_remote_copy(
            src_ref=stored(0, k, up), dst_ref=X.at[k], send_sem=semOs.at[k], recv_sem=semXr.at[k],
            device_id=at(dy=jnp.where(up, 3, 1), other_core=jnp.where(up, 0, 1)), device_id_type=MESH,
        )

    def detour_out(k):
        n = number(k, up_core)
        return pltpu.make_async_remote_copy(
            src_ref=X.at[k], dst_ref=piece(0, k, up_core), send_sem=semXs.at[k], recv_sem=semLr.at[0, n],
            device_id=at(dx=jnp.where(up_core, 1, 3)), device_id_type=MESH,
        )

    lends = jnp.logical_and(own_core, jnp.logical_or(d == 1, d == 3))
    lends_up = d == 1

    def load_row(s):
        return pltpu.make_async_copy(anc.at[s], A.at[s], semA.at[s])

    small = [
        pltpu.make_async_copy(f1, Fl.at[:, 0], semF.at[0]),
        pltpu.make_async_copy(f2, Fl.at[:, 1], semF.at[1]),
        pltpu.make_async_copy(link, lk, semF.at[2]),
        pltpu.make_async_copy(inv1, i1, semF.at[3]),
        pltpu.make_async_copy(inv2, i2, semF.at[4]),
    ]
    barrier = pltpu.get_barrier_semaphore()
    partners = [at(other_core=1 - core), at(dx=1), at(dx=3), at(dz=1), at(dz=3), at(dy=2)]
    for o in (1, 3):
        partners += [at(dy=o), at(dy=o, other_core=1 - core)]
    for partner in partners:
        pl.semaphore_signal(barrier, inc=1, device_id=partner, device_id_type=MESH)

    for copy in small:
        copy.start()

    @pl.when(is_src)
    def _():
        for p in range(2):

            @pl.loop(0, 8)
            def _(k):
                for up in (True, False):
                    local_piece(p, k, up).start()

    for s in range(16):
        load_row(s).start()
    pl.semaphore_wait(barrier, len(partners))

    for p in range(2):

        @pl.when(is_src)
        def _():
            @pl.loop(0, 8)
            def _(k):
                for up in (True, False):
                    along(p, k, up, stored(p, k, up)).start()

        if p == 0:

            @pl.when(lends)
            def _():
                @pl.loop(0, 8)
                def _(k):
                    detour_in(k, lends_up).start()

    @pl.when(is_src)
    def _():
        for p in range(2):

            @pl.loop(0, 8)
            def _(k):
                for up in (True, False):
                    across(p, k, up, stored(p, k, up)).start()

    for copy in small:
        copy.wait()

    @pl.loop(0, 16)
    def _(s):
        two = jnp.full((T, T), m2[16 * r + s].astype(F32), F32).astype(BF16)
        Fl[s, 0] = Fl[s, 0].T
        Fl[s, 1] = (Fl[s, 1] * two).T

    def relay(p, k):
        @pl.when(inside)
        def _():
            across(p, k, up_core).wait_recv()

            @pl.when(onward[p])
            def _():
                along(p, k, up_core, piece(p, k, up_core)).start()

            across(p, k, up_core).start()

        if p == 0:

            @pl.when(d == 0)
            def _():
                detour_in(k, up_core).wait_recv()
                detour_out(k).start()

    def arrived(p):
        @pl.loop(0, 8)
        def _(k):
            @pl.when(inside)
            def _():
                across(p, k, down_core).wait_recv()

            @pl.when(is_src)
            def _():
                for up in (True, False):
                    local_piece(p, k, up).wait()

            @pl.when(fed)
            def _():
                for up in (True, False):
                    across(p, k, up).wait_recv()

    def factors_left(p):
        @pl.loop(0, 8)
        def _(k):
            @pl.when(is_src)
            def _():
                for up in (True, False):
                    along(p, k, up, stored(p, k, up)).wait_send()
                    across(p, k, up).wait_send()

            if p == 0:

                @pl.when(lends)
                def _():
                    detour_in(k, lends_up).wait_send()

                @pl.when(d == 0)
                def _():
                    detour_out(k).wait_send()

            @pl.when(onward[p])
            def _():
                along(p, k, up_core, piece(p, k, up_core)).wait_send()

            @pl.when(inside)
            def _():
                across(p, k, up_core).wait_send()

    def slot(h, du, dv):
        dx, dz = (du, dv) if h == 0 else (dv, du)
        return ((x + dx) % 4) * 4 + (z + dz) % 4

    def rs_copy(p, h, way, m, src, dst):
        step = 1 if way == 0 else 3
        device = at(dx=step) if h == 0 else at(dz=step)
        return pltpu.make_async_remote_copy(
            src_ref=src, dst_ref=dst, send_sem=ssem.at[p, h, way, m], recv_sem=rsem.at[p, h, way, m],
            device_id=device, device_id_type=MESH,
        )

    def rows_of(h):
        return pl.ds(h * half, half)

    def first_hop(p, h, way, k, src=None):
        return rs_copy(p, h, way, k, B1.at[p, h, way, k] if src is None else src, B1.at[p, h, way, k])

    def second_hop(p, h, way, dv, src=None):
        return rs_copy(p, h, way, 2 + dv, B2.at[p, h, way, dv] if src is None else src, B2.at[p, h, way, dv])

    def third_hop(p, h, dv):
        device = at(dz=dv) if h == 0 else at(dx=dv)
        return pltpu.make_async_remote_copy(
            src_ref=B2.at[p, h, 0, dv], dst_ref=C.at[p, h, dv - 1],
            send_sem=ssem.at[p, h, 0, 5 + dv], recv_sem=rsem.at[p, h, 0, 5 + dv],
            device_id=device, device_id_type=MESH,
        )

    def product(p, pair):
        places, weights = [], []
        for e in range(2):
            i = 2 * pair + e
            dx, dz = pick(i, [v[0] for v in ORDER]), pick(i, [v[1] for v in ORDER])
            s = ((x + dx) % 4) * 4 + (z + dz) % 4
            places.append((dx, dz, s))
            weights.append(members[p][16 * r + s])
        acc = None
        for j in range(8):
            other = members[p][8 * c + j]
            a = [masked(A[s, j], tm[j, s] * own * other) for (_, _, s), own in zip(places, weights)]
            term = jnp.dot(jnp.concatenate(a, 0), L[p, j], preferred_element_type=F32)
            acc = term if acc is None else acc + term
        for e, (dx, dz, s) in enumerate(places):
            Pb[p, s] = acc[e * T : (e + 1) * T].astype(BF16)
        for dx, dz, s in places:
            send_on(p, dx, dz, s)

    def masked(a, w):
        return a * jnp.full((T, T), w.astype(F32), F32).astype(BF16)

    def send_on(p, dx, dz, s):
        for h in range(2):
            du, dv = (dx, dz) if h == 0 else (dz, dx)
            inner = jnp.logical_or(dv == 1, dv == 2)
            outer = jnp.logical_not(inner)
            src = Pb.at[p, s, rows_of(h)]

            @pl.when(jnp.logical_and(du == 2, inner))
            def _():
                first_hop(p, h, 0, dv - 1, src).start()

            @pl.when(jnp.logical_and(du == 2, outer))
            def _():
                first_hop(p, h, 1, dv // 3, src).start()

            @pl.when(jnp.logical_and(du == 1, outer))
            def _():
                second_hop(p, h, 0, dv, src).start()

            @pl.when(jnp.logical_and(du == 3, inner))
            def _():
                second_hop(p, h, 1, dv, src).start()

    def add_and_pass(p):
        for k in range(2):
            for h in range(2):
                for way in range(2):
                    du, dv = (1, k + 1) if way == 0 else (3, 3 * k)
                    first_hop(p, h, way, k).wait_recv()
                    mine = Pb[p, slot(h, du, dv), rows_of(h)].astype(F32)
                    B1[p, h, way, k] = (mine + B1[p, h, way, k].astype(F32)).astype(BF16)
                    second_hop(p, h, way, dv, B1.at[p, h, way, k]).start()

    def line_sum(p, h, dv):
        for way in range(2):
            second_hop(p, h, way, dv).wait_recv()
        total = Pb[p, slot(h, 0, dv), rows_of(h)].astype(F32)
        return total + B2[p, h, 0, dv].astype(F32) + B2[p, h, 1, dv].astype(F32)

    def stage_two(p, dv):
        for h in range(2):
            B2[p, h, 0, dv] = line_sum(p, h, dv).astype(BF16)
            third_hop(p, h, dv).start()

    def stage_two_own(p):
        for h in range(2):
            R[p, rows_of(h)] = line_sum(p, h, 0)

    def stage_two_end(p):
        for h in range(2):
            total = R[p, rows_of(h)]
            for dv in range(1, 4):
                third_hop(p, h, dv).wait_recv()
                total += C[p, h, dv - 1].astype(F32)
            R[p, rows_of(h)] = total

    def contract():
        @pl.loop(0, 4)
        def _(q):
            total = None
            for t in range(4):
                left = Fl[4 * q + t].reshape(2 * T, T)
                term = jnp.dot(left, Pb[0, 4 * q + t], preferred_element_type=F32)
                total = term if total is None else total + term
            pieces = [total[k * T : (k + 1) * T].reshape(32, sub, T) for k in range(2)]

            @pl.when(q == 0)
            def _():
                for k in range(2):
                    Gf[:, k] = pieces[k]

            @pl.when(q > 0)
            def _():
                for k in range(2):
                    Gf[:, k] += pieces[k]

    def from_left(t):
        q, j = t // 8, t % 8
        total = None
        for k in range(8):
            s = 8 * q + k
            term = jnp.dot(Fl[s, 1], masked(A[s, j], tm[j, s]), preferred_element_type=F32)
            total = term if total is None else total + term

        @pl.when(q == 0)
        def _():
            U[j] = total

        @pl.when(q > 0)
        def _():
            U[j] += total

    def finish_from_left():
        total = None
        for j in range(8):
            left = U[j].astype(BF16)
            term = jnp.dot(left, masked(L[1, j], m2[8 * c + j]), preferred_element_type=F32)
            total = term if total is None else total + term
        Gf[:, 2] = total.reshape(32, sub, T)

    @pl.loop(0, 16)
    def _(t):
        @pl.when(jnp.logical_and(early, jnp.logical_and(t >= 3, t < 11)))
        def _():
            relay(0, t - 3)

        @pl.when(jnp.logical_and(away == 1, jnp.logical_and(t >= 11, t < 15)))
        def _():
            relay(1, t - 11)

        @pl.when(jnp.logical_and(jnp.logical_not(early), t >= 8))
        def _():
            relay(0, t - 8)

        @pl.when(t % 8 == 0)
        def _():
            for k in range(8):
                load_row(t + k).wait()

        from_left(t)

    arrived(0)

    @pl.loop(0, 8)
    def _(i):
        product(0, i)

        @pl.when(away == 2)
        def _():
            relay(1, i)

        @pl.when(jnp.logical_and(away == 1, i < 4))
        def _():
            relay(1, 4 + i)

    add_and_pass(0)
    def last_hop(first):
        @pl.when(away == 3)
        def _():
            @pl.loop(first, first + 4)
            def _(k):
                relay(1, k)

    last_hop(0)
    contract()
    last_hop(4)
    arrived(1)
    finish_from_left()
    Gs[...] = Gf[...].astype(BF16)

    def out_copy(k):
        return pltpu.make_async_copy(O.at[k], (o1.at[0], o2.at[0], od1, oc, od2)[k], semO.at[k])

    def put(k, value):
        O[k] = value
        out_copy(k).start()

    def g_copy(o, src, dst, device):
        return pltpu.make_async_remote_copy(
            src_ref=src, dst_ref=dst, send_sem=gsend.at[o], recv_sem=grecv.at[o],
            device_id=device, device_id_type=MESH,
        )

    g = core * 16 + y * 4 + x
    plane = [(a, b) for a in range(4) for b in range(4) if (a, b) != (0, 0)]
    g_pair = g_copy(0, Gs.at[pl.ds((1 - core) * 16, 16)], Gr1, at(other_core=1 - core))
    b_pair = g_copy(16, Fin.at[pl.ds(core * 16, 16)], Fin.at[pl.ds(core * 16, 16)], at(other_core=1 - core))
    g_plane, b_plane = [], []
    for a, b in plane:
        n = 4 * a + b
        src = Hb.at[(y + b) % 4 * 4 + (x + a) % 4]
        g_plane.append(g_copy(n, src, Gr2.at[n], at(dx=a, dy=b)))
        b_plane.append(g_copy(16 + n, Fin.at[g], Fin.at[g], at(dx=a, dy=b)))
    g_z = [g_copy(31 + o, Jb.at[z], Jb.at[z], at(dz=o)) for o in range(1, 4)]

    g_pair.start()

    @pl.loop(0, 8)
    def _(i):
        product(1, i)

        @pl.when(i == 2)
        def _():
            stage_two(0, 2)
            g_pair.wait_recv()
            Hb[...] = (Gf[pl.ds(core * 16, 16)] + Gr1[...].astype(F32)).astype(BF16)
            for copy in g_plane:
                copy.start()

    add_and_pass(1)
    stage_two(0, 1)
    stage_two(0, 3)
    stage_two_own(0)
    for copy in g_plane:
        copy.wait_recv()
    total = Hb[y * 4 + x].astype(F32)
    for a, b in plane:
        total += Gr2[4 * a + b].astype(F32)
    Jb[z] = total.astype(BF16)
    for copy in g_z:
        copy.start()
    for copy in g_z:
        copy.wait_recv()
    total = Jb[0].astype(F32)
    for o in range(1, 4):
        total += Jb[o].astype(F32)
    rows = pl.ds(pl.multiple_of(g * sub, sub), sub)
    Fin[g, 0] = (i1[rows] + total[0]).astype(BF16)
    Fin[g, 1] = total[1].astype(BF16)
    Fin[g, 2] = (i2[rows] + total[2]).astype(BF16)
    for copy in b_plane:
        copy.start()
    stage_two_end(0)
    for dv in (2, 1, 3):
        stage_two(1, dv)
    col = (-R[0]).astype(BF16)
    put(0, col)
    R[0] = jnp.dot(col, lk[...], preferred_element_type=F32) * m2[16 * r + c].astype(F32)
    stage_two_own(1)
    for copy in b_plane:
        copy.wait_recv()
    b_pair.start()
    stage_two_end(1)
    put(1, (-(R[1] + R[0])).astype(BF16))
    b_pair.wait_recv()
    d1 = Fin[:, 0].astype(F32).reshape(T, T).astype(BF16)
    s21 = Fin[:, 1].astype(F32).reshape(T, T)
    put(2, d1)
    cross = (s21.T - jnp.dot(d1, lk[...], preferred_element_type=F32)).astype(BF16)
    put(3, cross)
    d2 = Fin[:, 2].astype(F32).reshape(T, T)
    d2 = d2 - jnp.dot(s21.astype(BF16), lk[...], preferred_element_type=F32)
    turned = lax.dot_general(lk[...], cross, (((0,), (0,)), ((), ())), preferred_element_type=F32)
    put(4, (d2 - turned).astype(BF16))

    for p in range(2):
        factors_left(p)
        for h in range(2):
            for dv in range(1, 4):
                third_hop(p, h, dv).wait_send()
            for way in range(2):
                for k in range(2):
                    first_hop(p, h, way, k).wait_send()
                for dv in range(4):
                    second_hop(p, h, way, dv).wait_send()
    for copy in [g_pair, *g_plane, *g_z, *b_plane, b_pair]:
        copy.wait_send()
    for k in range(5):
        out_copy(k).wait()


def hand_on(*refs):
    for k in range(5):
        refs[5 + k][...] = refs[k][...]


def shards(anc, tm, m1, m2, f1, f2, link, inv1, inv2):
    T = anc.shape[2]
    half, sub = T // 2, T // 32
    any_space = pl.BlockSpec(memory_space=pltpu.HBM)
    smem = pl.BlockSpec(memory_space=pltpu.SMEM)
    vmem = pl.BlockSpec(memory_space=pltpu.VMEM)
    dma = pltpu.SemaphoreType.DMA
    tile = jax.ShapeDtypeStruct((T, T), BF16)
    column = jax.ShapeDtypeStruct((1, T, T), BF16)
    parts = pl.pallas_call(
        kernel,
        out_shape=(column, column, tile, tile, tile),
        in_specs=[any_space, smem, smem, smem, any_space, any_space, any_space, any_space, any_space],
        out_specs=(any_space,) * 5,
        scratch_shapes=[
            pltpu.VMEM((5, T, T), BF16),
            dma((5,)),
            pltpu.VMEM((16, 8, T, T), BF16),
            pltpu.VMEM((2, 8, T, T), BF16),
            pltpu.VMEM((8, half, T), BF16),
            pltpu.VMEM((16, 2, T, T), BF16),
            pltpu.VMEM((8, T, T), F32),
            pltpu.VMEM((2, 16, T, T), BF16),
            pltpu.VMEM((2, 2, 2, 2, half, T), BF16),
            pltpu.VMEM((2, 2, 2, 4, half, T), BF16),
            pltpu.VMEM((2, 2, 3, half, T), BF16),
            pltpu.VMEM((2, T, T), F32),
            pltpu.VMEM((32, 3, sub, T), F32),
            pltpu.VMEM((32, 3, sub, T), BF16),
            pltpu.VMEM((16, 3, sub, T), BF16),
            pltpu.VMEM((16, 3, sub, T), BF16),
            pltpu.VMEM((16, 3, sub, T), BF16),
            pltpu.VMEM((4, 3, sub, T), BF16),
            pltpu.VMEM((32, 3, sub, T), BF16),
            pltpu.VMEM((T, T), BF16),
            pltpu.VMEM((T, T), F32),
            pltpu.VMEM((T, T), F32),
            dma((16,)),
            dma((5,)),
            dma((2, 16)),
            dma((2, 16)),
            dma((2, 16)),
            dma((8,)),
            dma((8,)),
            dma((8,)),
            dma((2, 2, 2, 9)),
            dma((2, 2, 2, 9)),
            dma((35,)),
            dma((35,)),
        ],
        compiler_params=pltpu.CompilerParams(
            collective_id=0, has_side_effects=True, vmem_limit_bytes=60 * 1024 * 1024
        ),
    )(anc, tm.T, m1, m2, f1, f2, link, inv1, inv2)
    return pl.pallas_call(
        hand_on,
        out_shape=(column, column, tile, tile, tile),
        in_specs=[vmem] * 5,
        out_specs=(vmem,) * 5,
    )(*parts)


def solution(mesh):
    in_specs = (
        P("row", "col", None, None),
        P("row", "col"),
        P(),
        P(),
        P("row", None, None),
        P("row", None, None),
        P(),
        P(),
        P(),
    )
    out_specs = (P(("row", "col"), None, None), P(("row", "col"), None, None), P(), P(), P())
    return jax.shard_map(shards, mesh=mesh, in_specs=in_specs, out_specs=out_specs, check_vma=False)
```

```python
import jax
import jax.numpy as jnp
from jax import lax
from jax.experimental import pallas as pl
from jax.experimental.pallas import tpu as pltpu
from jax.sharding import PartitionSpec as P

MESH = pl.DeviceIdType.MESH
F32 = jnp.float32
BF16 = jnp.bfloat16
ORDER = (
    (2, 2), (2, 1), (1, 2), (2, 0), (0, 2), (2, 3), (3, 2), (1, 3),
    (3, 1), (1, 0), (0, 1), (1, 1), (3, 3), (3, 0), (0, 3), (0, 0),
)


def pick(index, values):
    out = jnp.int32(values[0])
    for k in range(1, len(values)):
        out = jnp.where(index == k, jnp.int32(values[k]), out)
    return out


def kernel(
    anc, tm, m1, m2, f1, f2, link, inv1, inv2,
    o1, o2, od1, oc, od2,
    O, semO, A, L, X, Fl, U, Pb, B1, B2, C, R, Gf, Gs, Gr1, Hb, Gr2, Ib, Gr3, Jb, Fin, lk, i1, i2,
    semA, semF, semLr, semLc, semLs, semXr, ssem, rsem1, rsem2, rsem3, gsend, grecv,
):
    T = anc.shape[2]
    half, sub = T // 2, T // 32
    r = lax.axis_index("row")
    c = lax.axis_index("col")
    y, core = r // 2, r % 2
    x, z = c // 4, c % 4

    def at(dx=0, dy=0, dz=0, other_core=None):
        which = core if other_core is None else other_core
        return {"row": ((y + dy) % 4) * 2 + which, "col": ((x + dx) % 4) * 4 + (z + dz) % 4}

    members = (m1, m2)

    def drain(ref, sem):
        pltpu.make_async_copy(ref, ref, sem).wait()


    d = (y + 4 - x) % 4
    own_core = core == z // 2
    off = 8 * (z % 2)
    is_src = jnp.logical_and(d == 0, own_core)
    inside = d != 0
    up_core = core == 0
    down_core = core == 1
    away = jnp.where(up_core, d, (4 - d) % 4)
    early = jnp.logical_or(away == 1, d == 0)

    def tile_of(k, up):
        return jnp.where(up, 0, 4) + k // 2

    def half_of(k):
        return pl.ds(k % 2 * half, half)

    def piece(p, k, up):
        return L.at[p, tile_of(k, up), half_of(k)]

    def stored(p, k, up):
        return (f1, f2)[p].at[off + tile_of(k, up), half_of(k)]

    def local_piece(p, k, up):
        return pltpu.make_async_copy(stored(p, k, up), piece(p, k, up), semLc.at[p])

    def along(p, k, up, src):
        return pltpu.make_async_remote_copy(
            src_ref=src, dst_ref=piece(p, k, up), send_sem=semLs.at[0], recv_sem=semLr.at[p, k],
            device_id=at(dy=jnp.where(up, 1, 3), other_core=jnp.where(up, 0, 1)), device_id_type=MESH,
        )

    def across(p, k, up, src=None):
        return pltpu.make_async_remote_copy(
            src_ref=piece(p, k, up) if src is None else src, dst_ref=piece(p, k, up),
            send_sem=semLs.at[1], recv_sem=semLc.at[p],
            device_id=at(other_core=1 - core), device_id_type=MESH,
        )

    def detour_in(k, up):
        return pltpu.make_async_remote_copy(
            src_ref=stored(0, k, up), dst_ref=X.at[k], send_sem=semLs.at[2], recv_sem=semXr.at[k],
            device_id=at(dy=jnp.where(up, 3, 1), other_core=jnp.where(up, 0, 1)), device_id_type=MESH,
        )

    def detour_out(k):
        return pltpu.make_async_remote_copy(
            src_ref=X.at[k], dst_ref=piece(0, k, up_core), send_sem=semLs.at[3], recv_sem=semLr.at[0, k],
            device_id=at(dx=jnp.where(up_core, 1, 3)), device_id_type=MESH,
        )

    def straight(k, up):
        return pltpu.make_async_remote_copy(
            src_ref=stored(1, k, up), dst_ref=piece(1, k, up), send_sem=semLs.at[4], recv_sem=semLr.at[1, k],
            device_id=at(dy=jnp.where(up, 3, 1), other_core=jnp.where(up, 0, 1)), device_id_type=MESH,
        )

    lends = jnp.logical_and(own_core, jnp.logical_or(d == 1, d == 3))
    lends_up = d == 1

    def load_row(s):
        return pltpu.make_async_copy(anc.at[s], A.at[s], semA.at[s // 8])

    small = [
        pltpu.make_async_copy(f1, Fl.at[:, 0], semF.at[0]),
        pltpu.make_async_copy(f2, Fl.at[:, 1], semF.at[0]),
        pltpu.make_async_copy(link, lk, semF.at[1]),
        pltpu.make_async_copy(inv1, i1, semF.at[2]),
        pltpu.make_async_copy(inv2, i2, semF.at[3]),
    ]
    barrier = pltpu.get_barrier_semaphore()
    partners = [at(other_core=1 - core), at(dx=1), at(dx=3), at(dz=1), at(dz=3), at(dy=2)]
    for o in (1, 3):
        partners += [at(dy=o), at(dy=o, other_core=1 - core)]
    for partner in partners:
        pl.semaphore_signal(barrier, inc=1, device_id=partner, device_id_type=MESH)

    for copy in small:
        copy.start()

    @pl.when(is_src)
    def _():
        for p in range(2):

            @pl.loop(0, 8)
            def _(k):
                for up in (True, False):
                    local_piece(p, k, up).start()

    for s in range(16):
        load_row(s).start()
    pl.semaphore_wait(barrier, len(partners))

    for p in range(2):

        @pl.when(is_src)
        def _():
            @pl.loop(0, 8)
            def _(k):
                for up in (True, False):
                    along(p, k, up, stored(p, k, up)).start()

        if p == 0:

            @pl.when(lends)
            def _():
                @pl.loop(0, 8)
                def _(k):
                    detour_in(k, lends_up).start()

        if p == 1:

            @pl.when(is_src)
            def _():
                @pl.loop(0, 8)
                def _(k):
                    for up in (True, False):
                        straight(k, up).start()

    @pl.when(is_src)
    def _():
        for p in range(2):

            @pl.loop(0, 8)
            def _(k):
                for up in (True, False):
                    across(p, k, up, stored(p, k, up)).start()

    drain(Fl, semF.at[0])
    for copy in small[2:]:
        copy.wait()

    @pl.loop(0, 16)
    def _(s):
        two = jnp.full((T, T), m2[16 * r + s].astype(F32), F32).astype(BF16)
        Fl[s, 0] = Fl[s, 0].T
        Fl[s, 1] = (Fl[s, 1] * two).T

    def relay(p, k):
        @pl.when(inside)
        def _():
            along(p, k, up_core, piece(p, k, up_core)).wait_recv()

            @pl.when(away == 1)
            def _():
                along(p, k, up_core, piece(p, k, up_core)).start()

            across(p, k, up_core).start()

        if p == 0:

            @pl.when(d == 0)
            def _():
                detour_in(k, up_core).wait_recv()
                detour_out(k).start()

    def arrived(p):
        @pl.when(inside)
        def _():
            drain(A.at[0, pl.ds(0, 4)], semLc.at[p])

        @pl.when(d == 0)
        def _():
            drain(A.at[0], semLc.at[p])

    def factors_left():
        @pl.when(is_src)
        def _():
            drain(A.at[pl.ds(0, 2)], semLs.at[0])
            drain(A.at[pl.ds(0, 2)], semLs.at[1])
            drain(A.at[0], semLs.at[4])

        @pl.when(away == 1)
        def _():
            drain(A.at[0], semLs.at[0])

        @pl.when(inside)
        def _():
            drain(A.at[0], semLs.at[1])

        @pl.when(lends)
        def _():
            drain(A.at[0, pl.ds(0, 4)], semLs.at[2])

        @pl.when(d == 0)
        def _():
            drain(A.at[0, pl.ds(0, 4)], semLs.at[3])

    def slot(h, du, dv):
        dx, dz = (du, dv) if h == 0 else (dv, du)
        return ((x + dx) % 4) * 4 + (z + dz) % 4

    def rs_copy(h, way, src, dst, sem):
        step = 1 if way == 0 else 3
        device = at(dx=step) if h == 0 else at(dz=step)
        return pltpu.make_async_remote_copy(
            src_ref=src, dst_ref=dst, send_sem=ssem.at[0], recv_sem=sem, device_id=device, device_id_type=MESH
        )

    def rows_of(h):
        return pl.ds(h * half, half)

    def first_hop(p, h, way, k, src):
        return rs_copy(h, way, src, B1.at[p, h, way, k], rsem1.at[p, h, way])

    def second_hop(p, h, way, dv, src):
        return rs_copy(h, way, src, B2.at[p, h, dv, way], rsem2.at[p, h, dv])

    def third_hop(p, h, dv):
        device = at(dz=dv) if h == 0 else at(dx=dv)
        return pltpu.make_async_remote_copy(
            src_ref=B2.at[p, h, dv, 0], dst_ref=C.at[p, h, dv - 1],
            send_sem=ssem.at[1], recv_sem=rsem3.at[p, h], device_id=device, device_id_type=MESH,
        )

    def product(p, pair):
        places, weights = [], []
        for e in range(2):
            i = 2 * pair + e
            dx, dz = pick(i, [v[0] for v in ORDER]), pick(i, [v[1] for v in ORDER])
            s = ((x + dx) % 4) * 4 + (z + dz) % 4
            places.append((dx, dz, s))
            weights.append(members[p][16 * r + s])
        acc = None
        for j in range(8):
            other = members[p][8 * c + j]
            a = [masked(A[s, j], tm[j, s] * own * other) for (_, _, s), own in zip(places, weights)]
            term = jnp.dot(jnp.concatenate(a, 0), L[p, j], preferred_element_type=F32)
            acc = term if acc is None else acc + term
        for e, (dx, dz, s) in enumerate(places):
            Pb[p, s] = acc[e * T : (e + 1) * T].astype(BF16)
        for dx, dz, s in places:
            send_on(p, dx, dz, s)

    def masked(a, w):
        return a * jnp.full((T, T), w.astype(F32), F32).astype(BF16)

    def send_on(p, dx, dz, s):
        for h in range(2):
            du, dv = (dx, dz) if h == 0 else (dz, dx)
            inner = jnp.logical_or(dv == 1, dv == 2)
            outer = jnp.logical_not(inner)
            src = Pb.at[p, s, rows_of(h)]

            @pl.when(jnp.logical_and(du == 2, inner))
            def _():
                first_hop(p, h, 0, dv - 1, src).start()

            @pl.when(jnp.logical_and(du == 2, outer))
            def _():
                first_hop(p, h, 1, dv // 3, src).start()

            @pl.when(jnp.logical_and(du == 1, outer))
            def _():
                second_hop(p, h, 0, dv, src).start()

            @pl.when(jnp.logical_and(du == 3, inner))
            def _():
                second_hop(p, h, 1, dv, src).start()

    def add_and_pass(p):
        for h in range(2):
            for way in range(2):
                drain(B1.at[p, h, way], rsem1.at[p, h, way])
                for k in range(2):
                    du, dv = (1, k + 1) if way == 0 else (3, 3 * k)
                    mine = Pb[p, slot(h, du, dv), rows_of(h)].astype(F32)
                    B1[p, h, way, k] = (mine + B1[p, h, way, k].astype(F32)).astype(BF16)
                    second_hop(p, h, way, dv, B1.at[p, h, way, k]).start()

    def line_sum(p, h, dv):
        drain(B2.at[p, h, dv], rsem2.at[p, h, dv])
        total = Pb[p, slot(h, 0, dv), rows_of(h)].astype(F32)
        return total + B2[p, h, dv, 0].astype(F32) + B2[p, h, dv, 1].astype(F32)

    def stage_two(p, dv):
        for h in range(2):
            B2[p, h, dv, 0] = line_sum(p, h, dv).astype(BF16)
            third_hop(p, h, dv).start()

    def stage_two_own(p):
        for h in range(2):
            R[p, rows_of(h)] = line_sum(p, h, 0)

    def stage_two_end(p):
        for h in range(2):
            total = R[p, rows_of(h)]
            drain(C.at[p, h], rsem3.at[p, h])
            for dv in range(1, 4):
                total += C[p, h, dv - 1].astype(F32)
            R[p, rows_of(h)] = total

    def contract():
        @pl.loop(0, 4)
        def _(q):
            total = None
            for t in range(4):
                left = Fl[4 * q + t].reshape(2 * T, T)
                term = jnp.dot(left, Pb[0, 4 * q + t], preferred_element_type=F32)
                total = term if total is None else total + term
            pieces = [total[k * T : (k + 1) * T].reshape(32, sub, T) for k in range(2)]

            @pl.when(q == 0)
            def _():
                for k in range(2):
                    Gf[:, k] = pieces[k]

            @pl.when(q > 0)
            def _():
                for k in range(2):
                    Gf[:, k] += pieces[k]

    def from_left(t):
        q, j = t // 8, t % 8
        total = None
        for k in range(8):
            s = 8 * q + k
            term = jnp.dot(Fl[s, 1], masked(A[s, j], tm[j, s]), preferred_element_type=F32)
            total = term if total is None else total + term

        @pl.when(q == 0)
        def _():
            U[j] = total

        @pl.when(q > 0)
        def _():
            U[j] += total

    def finish_from_left():
        total = None
        for j in range(8):
            left = U[j].astype(BF16)
            term = jnp.dot(left, masked(L[1, j], m2[8 * c + j]), preferred_element_type=F32)
            total = term if total is None else total + term
        Gf[:, 2] = total.reshape(32, sub, T)

    @pl.loop(0, 16)
    def _(t):
        @pl.when(jnp.logical_and(early, jnp.logical_and(t >= 3, t < 11)))
        def _():
            relay(0, t - 3)

        @pl.when(jnp.logical_and(away == 1, jnp.logical_and(t >= 11, t < 15)))
        def _():
            relay(1, t - 11)

        @pl.when(jnp.logical_and(jnp.logical_not(early), t >= 8))
        def _():
            relay(0, t - 8)

        @pl.when(t % 8 == 0)
        def _():
            drain(A.at[pl.ds(0, 8)], semA.at[t // 8])

        from_left(t)

    arrived(0)

    @pl.loop(0, 8)
    def _(i):
        product(0, i)

        @pl.when(away == 2)
        def _():
            relay(1, i)

        @pl.when(jnp.logical_and(away == 3, i >= 4))
        def _():
            relay(1, i - 4)

        @pl.when(jnp.logical_and(away == 1, i < 4))
        def _():
            relay(1, 4 + i)

    contract()

    @pl.when(away == 3)
    def _():
        @pl.loop(4, 8)
        def _(k):
            relay(1, k)

    add_and_pass(0)
    arrived(1)
    finish_from_left()
    Gs[...] = Gf[...].astype(BF16)

    def out_copy(k):
        return pltpu.make_async_copy(O.at[k], (o1.at[0], o2.at[0], od1, oc, od2)[k], semO.at[0])

    def put(k, value):
        O[k] = value
        out_copy(k).start()

    def g_copy(kind, src, dst, device):
        return pltpu.make_async_remote_copy(
            src_ref=src, dst_ref=dst, send_sem=gsend.at[kind], recv_sem=grecv.at[kind],
            device_id=device, device_id_type=MESH,
        )

    g = core * 16 + y * 4 + x
    plane = [(a, b) for a in range(4) for b in range(4) if (a, b) != (0, 0)]
    g_pair = g_copy(0, Gs.at[pl.ds((1 - core) * 16, 16)], Gr1, at(other_core=1 - core))
    b_pair = g_copy(5, Fin.at[pl.ds(core * 16, 16)], Fin.at[pl.ds(core * 16, 16)], at(other_core=1 - core))
    b_plane = []
    for a, b in plane:
        b_plane.append(g_copy(4, Fin.at[g], Fin.at[g], at(dx=a, dy=b)))
    g_y = [g_copy(1, Hb.at[pl.ds((y + o) % 4 * 4, 4)], Gr2.at[o - 1], at(dy=o)) for o in range(1, 4)]
    g_x = [g_copy(2, Ib.at[(x + o) % 4], Gr3.at[o - 1], at(dx=o)) for o in range(1, 4)]
    g_z = [g_copy(3, Jb.at[z], Jb.at[z], at(dz=o)) for o in range(1, 4)]

    g_pair.start()

    @pl.loop(0, 8)
    def _(i):
        product(1, i)

        @pl.when(i == 0)
        def _():
            g_pair.wait_recv()
            Hb[...] = (Gf[pl.ds(core * 16, 16)] + Gr1[...].astype(F32)).astype(BF16)
            for copy in g_y:
                copy.start()

        @pl.when(i == 6)
        def _():
            drain(Gr2, grecv.at[1])
            total = Hb[pl.ds(y * 4, 4)].astype(F32)
            for o in range(3):
                total += Gr2[o].astype(F32)
            Ib[...] = total.astype(BF16)
            stage_two(0, 2)
            for copy in g_x:
                copy.start()

    add_and_pass(1)
    stage_two(0, 1)
    stage_two(0, 3)
    stage_two_own(0)
    drain(Gr3, grecv.at[2])
    total = Ib[x].astype(F32)
    for o in range(3):
        total += Gr3[o].astype(F32)
    Jb[z] = total.astype(BF16)
    for copy in g_z:
        copy.start()
    drain(Jb.at[pl.ds(0, 3)], grecv.at[3])
    total = Jb[0].astype(F32)
    for o in range(1, 4):
        total += Jb[o].astype(F32)
    rows = pl.ds(pl.multiple_of(g * sub, sub), sub)
    Fin[g, 0] = (i1[rows] + total[0]).astype(BF16)
    Fin[g, 1] = total[1].astype(BF16)
    Fin[g, 2] = (i2[rows] + total[2]).astype(BF16)
    for copy in b_plane:
        copy.start()
    stage_two_end(0)
    for dv in (2, 1, 3):
        stage_two(1, dv)
    col = (-R[0]).astype(BF16)
    put(0, col)
    R[0] = jnp.dot(col, lk[...], preferred_element_type=F32) * m2[16 * r + c].astype(F32)
    stage_two_own(1)
    drain(Fin.at[pl.ds(0, 15)], grecv.at[4])
    b_pair.start()
    stage_two_end(1)
    put(1, (-(R[1] + R[0])).astype(BF16))
    b_pair.wait_recv()
    d1 = Fin[:, 0].astype(F32).reshape(T, T).astype(BF16)
    s21 = Fin[:, 1].astype(F32).reshape(T, T)
    put(2, d1)
    cross = (s21.T - jnp.dot(d1, lk[...], preferred_element_type=F32)).astype(BF16)
    put(3, cross)
    d2 = Fin[:, 2].astype(F32).reshape(T, T)
    d2 = d2 - jnp.dot(s21.astype(BF16), lk[...], preferred_element_type=F32)
    turned = lax.dot_general(lk[...], cross, (((0,), (0,)), ((), ())), preferred_element_type=F32)
    put(4, (d2 - turned).astype(BF16))

    factors_left()
    drain(A.at[pl.ds(0, 3)], ssem.at[0])
    drain(A.at[0, pl.ds(0, 6)], ssem.at[1])
    g_pair.wait_send()
    drain(Gr2, gsend.at[1])
    drain(Gr3, gsend.at[2])
    drain(Jb.at[pl.ds(0, 3)], gsend.at[3])
    drain(Fin.at[pl.ds(0, 15)], gsend.at[4])
    b_pair.wait_send()
    drain(O, semO.at[0])


def hand_on(*refs):
    for k in range(5):
        refs[5 + k][...] = refs[k][...]


def shards(anc, tm, m1, m2, f1, f2, link, inv1, inv2):
    T = anc.shape[2]
    half, sub = T // 2, T // 32
    any_space = pl.BlockSpec(memory_space=pltpu.HBM)
    smem = pl.BlockSpec(memory_space=pltpu.SMEM)
    vmem = pl.BlockSpec(memory_space=pltpu.VMEM)
    dma = pltpu.SemaphoreType.DMA
    tile = jax.ShapeDtypeStruct((T, T), BF16)
    column = jax.ShapeDtypeStruct((1, T, T), BF16)
    parts = pl.pallas_call(
        kernel,
        out_shape=(column, column, tile, tile, tile),
        in_specs=[any_space, smem, smem, smem, any_space, any_space, any_space, any_space, any_space],
        out_specs=(any_space,) * 5,
        scratch_shapes=[
            pltpu.VMEM((5, T, T), BF16),
            dma((1,)),
            pltpu.VMEM((16, 8, T, T), BF16),
            pltpu.VMEM((2, 8, T, T), BF16),
            pltpu.VMEM((8, half, T), BF16),
            pltpu.VMEM((16, 2, T, T), BF16),
            pltpu.VMEM((8, T, T), F32),
            pltpu.VMEM((2, 16, T, T), BF16),
            pltpu.VMEM((2, 2, 2, 2, half, T), BF16),
            pltpu.VMEM((2, 2, 4, 2, half, T), BF16),
            pltpu.VMEM((2, 2, 3, half, T), BF16),
            pltpu.VMEM((2, T, T), F32),
            pltpu.VMEM((32, 3, sub, T), F32),
            pltpu.VMEM((32, 3, sub, T), BF16),
            pltpu.VMEM((16, 3, sub, T), BF16),
            pltpu.VMEM((16, 3, sub, T), BF16),
            pltpu.VMEM((3, 4, 3, sub, T), BF16),
            pltpu.VMEM((4, 3, sub, T), BF16),
            pltpu.VMEM((3, 3, sub, T), BF16),
            pltpu.VMEM((4, 3, sub, T), BF16),
            pltpu.VMEM((32, 3, sub, T), BF16),
            pltpu.VMEM((T, T), BF16),
            pltpu.VMEM((T, T), F32),
            pltpu.VMEM((T, T), F32),
            dma((2,)),
            dma((4,)),
            dma((2, 8)),
            dma((2,)),
            dma((5,)),
            dma((8,)),
            dma((2,)),
            dma((2, 2, 2)),
            dma((2, 2, 4)),
            dma((2, 2)),
            dma((6,)),
            dma((6,)),
        ],
        compiler_params=pltpu.CompilerParams(
            collective_id=0, has_side_effects=True, vmem_limit_bytes=60 * 1024 * 1024
        ),
    )(anc, tm.T, m1, m2, f1, f2, link, inv1, inv2)
    return pl.pallas_call(
        hand_on,
        out_shape=(column, column, tile, tile, tile),
        in_specs=[vmem] * 5,
        out_specs=(vmem,) * 5,
    )(*parts)


def solution(mesh):
    in_specs = (
        P("row", "col", None, None),
        P("row", "col"),
        P(),
        P(),
        P("row", None, None),
        P("row", None, None),
        P(),
        P(),
        P(),
    )
    out_specs = (P(("row", "col"), None, None), P(("row", "col"), None, None), P(), P(), P())
    return jax.shard_map(shards, mesh=mesh, in_specs=in_specs, out_specs=out_specs, check_vma=False)
```

```python
import jax
import jax.numpy as jnp
from jax import lax
from jax.experimental import pallas as pl
from jax.experimental.pallas import tpu as pltpu
from jax.sharding import PartitionSpec as P

MESH = pl.DeviceIdType.MESH
F32 = jnp.float32
BF16 = jnp.bfloat16
ORDER = (
    (2, 2), (2, 1), (1, 2), (2, 0), (0, 2), (2, 3), (3, 2), (1, 3),
    (3, 1), (1, 0), (0, 1), (1, 1), (3, 3), (3, 0), (0, 3), (0, 0),
)


def pick(index, values):
    out = jnp.int32(values[0])
    for k in range(1, len(values)):
        out = jnp.where(index == k, jnp.int32(values[k]), out)
    return out


def kernel(
    anc, tm, m1, m2, f1, f2, link, inv1, inv2,
    o1, o2, od1, oc, od2,
    O, semO, A, L, X, Y, Fl, U, Pb, B1, B2, C, R, Gf, Gs, Gr1, Hb, Gr2, Ib, Gr3, Jb, Fin, lk, i1, i2,
    semA, semF, semLr, semLc, semLs, semXr, semY, ssem, rsem0, rsem1, rsem2, rsem3, gsend, grecv,
):
    T = anc.shape[2]
    half, sub = T // 2, T // 32
    r = lax.axis_index("row")
    c = lax.axis_index("col")
    y, core = r // 2, r % 2
    x, z = c // 4, c % 4

    def at(dx=0, dy=0, dz=0, other_core=None):
        which = core if other_core is None else other_core
        return {"row": ((y + dy) % 4) * 2 + which, "col": ((x + dx) % 4) * 4 + (z + dz) % 4}

    members = (m1, m2)

    def drain(ref, sem):
        pltpu.make_async_copy(ref, ref, sem).wait()


    d = (y + 4 - x) % 4
    own_core = core == z // 2
    off = 8 * (z % 2)
    is_src = jnp.logical_and(d == 0, own_core)
    inside = d != 0
    up_core = core == 0
    down_core = core == 1
    away = jnp.where(up_core, d, (4 - d) % 4)
    early = jnp.logical_or(away == 1, d == 0)

    def tile_of(k, up):
        return jnp.where(up, 0, 4) + k // 2

    def half_of(k):
        return pl.ds(k % 2 * half, half)

    def piece(p, k, up):
        return L.at[p, tile_of(k, up), half_of(k)]

    def stored(p, k, up):
        return (f1, f2)[p].at[off + tile_of(k, up), half_of(k)]

    def local_piece(p, k, up):
        return pltpu.make_async_copy(stored(p, k, up), piece(p, k, up), semLc.at[p])

    def along(p, k, up, src):
        return pltpu.make_async_remote_copy(
            src_ref=src, dst_ref=piece(p, k, up), send_sem=semLs.at[0], recv_sem=semLr.at[p, k],
            device_id=at(dy=jnp.where(up, 1, 3), other_core=jnp.where(up, 0, 1)), device_id_type=MESH,
        )

    def across(p, k, up):
        return pltpu.make_async_remote_copy(
            src_ref=piece(p, k, up), dst_ref=piece(p, k, up),
            send_sem=semLs.at[1], recv_sem=semLc.at[p],
            device_id=at(other_core=1 - core), device_id_type=MESH,
        )

    def detour_in(k, up):
        return pltpu.make_async_remote_copy(
            src_ref=Y.at[k], dst_ref=X.at[k], send_sem=semLs.at[2], recv_sem=semXr.at[k],
            device_id=at(dy=jnp.where(up, 3, 1), other_core=jnp.where(up, 0, 1)), device_id_type=MESH,
        )

    def detour_out(k):
        return pltpu.make_async_remote_copy(
            src_ref=X.at[k], dst_ref=piece(0, k, up_core), send_sem=semLs.at[3], recv_sem=semLr.at[0, k],
            device_id=at(dx=jnp.where(up_core, 1, 3)), device_id_type=MESH,
        )

    def straight(k, up):
        return pltpu.make_async_remote_copy(
            src_ref=piece(1, k, up), dst_ref=piece(1, k, up), send_sem=semLs.at[4], recv_sem=semLr.at[1, k],
            device_id=at(dy=jnp.where(up, 3, 1), other_core=jnp.where(up, 0, 1)), device_id_type=MESH,
        )

    lends = jnp.logical_and(own_core, jnp.logical_or(d == 1, d == 3))
    lends_up = d == 1

    def load_row(s):
        return pltpu.make_async_copy(anc.at[s], A.at[s], semA.at[s // 8])

    small = [
        pltpu.make_async_copy(f1, Fl.at[:, 0], semF.at[0]),
        pltpu.make_async_copy(f2, Fl.at[:, 1], semF.at[0]),
        pltpu.make_async_copy(link, lk, semF.at[1]),
        pltpu.make_async_copy(inv1, i1, semF.at[2]),
        pltpu.make_async_copy(inv2, i2, semF.at[3]),
    ]
    barrier = pltpu.get_barrier_semaphore()
    partners = [at(other_core=1 - core), at(dx=1), at(dx=3), at(dz=1), at(dz=3), at(dx=2), at(dy=2), at(dz=2)]
    for o in (1, 3):
        partners += [at(dy=o), at(dy=o, other_core=1 - core)]
    for partner in partners:
        pl.semaphore_signal(barrier, inc=1, device_id=partner, device_id_type=MESH)

    def lent(k):
        return pltpu.make_async_copy(stored(0, k, lends_up), Y.at[k], semY.at[0])

    @pl.when(lends)
    def _():
        @pl.loop(0, 8)
        def _(k):
            lent(k).start()

    for p in range(2):

        @pl.when(is_src)
        def _():
            @pl.loop(0, 8)
            def _(k):
                for up in (True, False):
                    local_piece(p, k, up).start()

        if p == 0:
            for copy in small:
                copy.start()

    for s in range(16):
        load_row(s).start()
    pl.semaphore_wait(barrier, len(partners))

    for p in range(2):

        @pl.when(is_src)
        def _():
            drain(A.at[0], semLc.at[p])

            @pl.loop(0, 8)
            def _(k):
                for up in (True, False):
                    along(p, k, up, piece(p, k, up)).start()

        if p == 0:

            @pl.when(lends)
            def _():
                drain(A.at[0, pl.ds(0, 4)], semY.at[0])

                @pl.loop(0, 8)
                def _(k):
                    detour_in(k, lends_up).start()

        if p == 1:

            @pl.when(is_src)
            def _():
                @pl.loop(0, 8)
                def _(k):
                    for up in (True, False):
                        straight(k, up).start()

    @pl.when(is_src)
    def _():
        for p in range(2):

            @pl.loop(0, 8)
            def _(k):
                for up in (True, False):
                    across(p, k, up).start()

    drain(Fl, semF.at[0])
    for copy in small[2:]:
        copy.wait()

    @pl.loop(0, 16)
    def _(s):
        two = jnp.full((T, T), m2[16 * r + s].astype(F32), F32).astype(BF16)
        Fl[s, 0] = Fl[s, 0].T
        Fl[s, 1] = (Fl[s, 1] * two).T

    def relay(p, k):
        @pl.when(inside)
        def _():
            along(p, k, up_core, piece(p, k, up_core)).wait_recv()

            @pl.when(away == 1)
            def _():
                along(p, k, up_core, piece(p, k, up_core)).start()

            across(p, k, up_core).start()

        if p == 0:

            @pl.when(d == 0)
            def _():
                detour_in(k, up_core).wait_recv()
                detour_out(k).start()

    def arrived(p):
        @pl.when(inside)
        def _():
            drain(A.at[0, pl.ds(0, 4)], semLc.at[p])

        @pl.when(jnp.logical_and(d == 0, jnp.logical_not(own_core)))
        def _():
            drain(A.at[0], semLc.at[p])

    def factors_left():
        @pl.when(is_src)
        def _():
            drain(A.at[pl.ds(0, 2)], semLs.at[0])
            drain(A.at[pl.ds(0, 2)], semLs.at[1])
            drain(A.at[0], semLs.at[4])

        @pl.when(away == 1)
        def _():
            drain(A.at[0], semLs.at[0])

        @pl.when(inside)
        def _():
            drain(A.at[0], semLs.at[1])

        @pl.when(lends)
        def _():
            drain(A.at[0, pl.ds(0, 4)], semLs.at[2])

        @pl.when(d == 0)
        def _():
            drain(A.at[0, pl.ds(0, 4)], semLs.at[3])

    def slot(h, du, dv):
        dx, dz = (du, dv) if h == 0 else (dv, du)
        return ((x + dx) % 4) * 4 + (z + dz) % 4

    def rs_copy(h, way, src, dst, sem):
        step = 1 if way == 0 else 3
        device = at(dx=step) if h == 0 else at(dz=step)
        return pltpu.make_async_remote_copy(
            src_ref=src, dst_ref=dst, send_sem=ssem.at[0], recv_sem=sem, device_id=device, device_id_type=MESH
        )

    def rows_of(h):
        return pl.ds(h * half, half)

    def first_hop(p, h, way, k, src):
        return rs_copy(h, way, src, B1.at[p, h, way, k], rsem1.at[p, h, way])

    def second_hop(p, h, way, dv, src):
        return rs_copy(h, way, src, B2.at[p, h, dv, way], rsem2.at[p, h, dv])

    def two_away(h, dv, src):
        device = at(dx=2) if h == 0 else at(dz=2)
        return pltpu.make_async_remote_copy(
            src_ref=src, dst_ref=B1.at[0, h, dv // 2, dv % 2],
            send_sem=ssem.at[0], recv_sem=rsem0.at[h, dv], device_id=device, device_id_type=MESH,
        )

    def third_hop(p, h, dv):
        device = at(dz=dv) if h == 0 else at(dx=dv)
        return pltpu.make_async_remote_copy(
            src_ref=B2.at[p, h, dv, 0], dst_ref=C.at[p, h, dv - 1],
            send_sem=ssem.at[1], recv_sem=rsem3.at[p, h], device_id=device, device_id_type=MESH,
        )

    def product(p, pair):
        places, weights = [], []
        for e in range(2):
            i = 2 * pair + e
            dx, dz = pick(i, [v[0] for v in ORDER]), pick(i, [v[1] for v in ORDER])
            s = ((x + dx) % 4) * 4 + (z + dz) % 4
            places.append((dx, dz, s))
            weights.append(members[p][16 * r + s])
        acc = None
        for j in range(8):
            other = members[p][8 * c + j]
            a = [masked(A[s, j], tm[j, s] * own * other) for (_, _, s), own in zip(places, weights)]
            term = jnp.dot(jnp.concatenate(a, 0), L[p, j], preferred_element_type=F32)
            acc = term if acc is None else acc + term
        for e, (dx, dz, s) in enumerate(places):
            Pb[p, s] = acc[e * T : (e + 1) * T].astype(BF16)
        for dx, dz, s in places:
            send_on(p, dx, dz, s)

    def masked(a, w):
        return a * jnp.full((T, T), w.astype(F32), F32).astype(BF16)

    def send_on(p, dx, dz, s):
        for h in range(2):
            du, dv = (dx, dz) if h == 0 else (dz, dx)
            inner = jnp.logical_or(dv == 1, dv == 2)
            outer = jnp.logical_not(inner)
            src = Pb.at[p, s, rows_of(h)]

            if p == 0:

                @pl.when(du == 1)
                def _():
                    second_hop(0, h, 0, dv, src).start()

                @pl.when(du == 3)
                def _():
                    second_hop(0, h, 1, dv, src).start()

                @pl.when(du == 2)
                def _():
                    two_away(h, dv, src).start()

                continue

            @pl.when(jnp.logical_and(du == 2, inner))
            def _():
                first_hop(p, h, 0, dv - 1, src).start()

            @pl.when(jnp.logical_and(du == 2, outer))
            def _():
                first_hop(p, h, 1, dv // 3, src).start()

            @pl.when(jnp.logical_and(du == 1, outer))
            def _():
                second_hop(p, h, 0, dv, src).start()

            @pl.when(jnp.logical_and(du == 3, inner))
            def _():
                second_hop(p, h, 1, dv, src).start()

    def add_and_pass(p):
        for h in range(2):
            for way in range(2):
                drain(B1.at[p, h, way], rsem1.at[p, h, way])
                for k in (1, 0):
                    du, dv = (1, k + 1) if way == 0 else (3, 3 * k)
                    mine = Pb[p, slot(h, du, dv), rows_of(h)].astype(F32)
                    B1[p, h, way, k] = (mine + B1[p, h, way, k].astype(F32)).astype(BF16)
                    second_hop(p, h, way, dv, B1.at[p, h, way, k]).start()

    def line_sum(p, h, dv):
        drain(B2.at[p, h, dv], rsem2.at[p, h, dv])
        total = Pb[p, slot(h, 0, dv), rows_of(h)].astype(F32)
        total += B2[p, h, dv, 0].astype(F32) + B2[p, h, dv, 1].astype(F32)
        if p == 0:
            drain(B1.at[0, h, dv // 2, dv % 2], rsem0.at[h, dv])
            total += B1[0, h, dv // 2, dv % 2].astype(F32)
        return total

    def stage_two_sum(p, dv):
        for h in range(2):
            B2[p, h, dv, 0] = line_sum(p, h, dv).astype(BF16)

    def stage_two(p, dv):
        stage_two_sum(p, dv)
        for h in range(2):
            third_hop(p, h, dv).start()

    def stage_two_own(p):
        for h in range(2):
            R[p, rows_of(h)] = line_sum(p, h, 0)

    def stage_two_end(p):
        for h in range(2):
            total = R[p, rows_of(h)]
            drain(C.at[p, h], rsem3.at[p, h])
            for dv in range(1, 4):
                total += C[p, h, dv - 1].astype(F32)
            R[p, rows_of(h)] = total

    def contract():
        @pl.loop(0, 4)
        def _(q):
            total = None
            for t in range(4):
                left = Fl[4 * q + t].reshape(2 * T, T)
                term = jnp.dot(left, Pb[0, 4 * q + t], preferred_element_type=F32)
                total = term if total is None else total + term
            pieces = [total[k * T : (k + 1) * T].reshape(32, sub, T) for k in range(2)]

            @pl.when(q == 0)
            def _():
                for k in range(2):
                    Gf[:, k] = pieces[k]

            @pl.when(q > 0)
            def _():
                for k in range(2):
                    Gf[:, k] += pieces[k]

    def from_left(t):
        q, j = t // 8, t % 8
        total = None
        for k in range(8):
            s = 8 * q + k
            term = jnp.dot(Fl[s, 1], masked(A[s, j], tm[j, s]), preferred_element_type=F32)
            total = term if total is None else total + term

        @pl.when(q == 0)
        def _():
            U[j] = total

        @pl.when(q > 0)
        def _():
            U[j] += total

    def finish_from_left():
        total = None
        for j in range(8):
            left = U[j].astype(BF16)
            term = jnp.dot(left, masked(L[1, j], m2[8 * c + j]), preferred_element_type=F32)
            total = term if total is None else total + term
        Gf[:, 2] = total.reshape(32, sub, T)

    @pl.loop(0, 16)
    def _(t):
        @pl.when(jnp.logical_and(early, jnp.logical_and(t >= 3, t < 11)))
        def _():
            relay(0, t - 3)

        @pl.when(jnp.logical_and(away == 1, jnp.logical_and(t >= 11, t < 15)))
        def _():
            relay(1, t - 11)

        @pl.when(jnp.logical_and(jnp.logical_not(early), t >= 8))
        def _():
            relay(0, t - 8)

        @pl.when(t % 8 == 0)
        def _():
            drain(A.at[pl.ds(0, 8)], semA.at[t // 8])

        from_left(t)

    arrived(0)

    @pl.loop(0, 8)
    def _(i):
        product(0, i)

        @pl.when(away == 2)
        def _():
            relay(1, i)

        @pl.when(jnp.logical_and(away == 3, i >= 4))
        def _():
            relay(1, i - 4)

        @pl.when(jnp.logical_and(away == 1, i < 4))
        def _():
            relay(1, 4 + i)

    contract()

    @pl.when(away == 3)
    def _():
        @pl.loop(4, 8)
        def _(k):
            relay(1, k)

    arrived(1)
    finish_from_left()
    Gs[...] = Gf[...].astype(BF16)

    def out_copy(k):
        return pltpu.make_async_copy(O.at[k], (o1.at[0], o2.at[0], od1, oc, od2)[k], semO.at[0])

    def put(k, value):
        O[k] = value
        out_copy(k).start()

    def g_copy(kind, src, dst, device):
        return pltpu.make_async_remote_copy(
            src_ref=src, dst_ref=dst, send_sem=gsend.at[kind], recv_sem=grecv.at[kind],
            device_id=device, device_id_type=MESH,
        )

    g = core * 16 + y * 4 + x
    plane = [(a, b) for a in range(4) for b in range(4) if (a, b) != (0, 0)]
    plane.sort(key=lambda v: -sum(min(e, 4 - e) for e in v))
    g_pair = g_copy(0, Gs.at[pl.ds((1 - core) * 16, 16)], Gr1, at(other_core=1 - core))
    b_pair = g_copy(5, Fin.at[pl.ds(core * 16, 16)], Fin.at[pl.ds(core * 16, 16)], at(other_core=1 - core))
    b_plane = []
    for a, b in plane:
        b_plane.append(g_copy(4, Fin.at[g], Fin.at[g], at(dx=a, dy=b)))
    g_y = [g_copy(1, Hb.at[pl.ds((y + o) % 4 * 4, 4)], Gr2.at[o - 1], at(dy=o)) for o in (2, 1, 3)]
    g_x = [g_copy(2, Ib.at[(x + o) % 4], Gr3.at[o - 1], at(dx=o)) for o in (2, 1, 3)]
    g_z = [g_copy(3, Jb.at[z], Jb.at[z], at(dz=o)) for o in (2, 1, 3)]

    g_pair.start()

    @pl.loop(0, 8)
    def _(i):
        product(1, i)

        @pl.when(i == 0)
        def _():
            g_pair.wait_recv()
            Hb[...] = (Gf[pl.ds(core * 16, 16)] + Gr1[...].astype(F32)).astype(BF16)
            for copy in g_y:
                copy.start()

        @pl.when(i == 6)
        def _():
            drain(Gr2, grecv.at[1])
            total = Hb[pl.ds(y * 4, 4)].astype(F32)
            for o in range(3):
                total += Gr2[o].astype(F32)
            Ib[...] = total.astype(BF16)
            stage_two_sum(0, 2)
            for copy in g_x:
                copy.start()
            for h in range(2):
                third_hop(0, h, 2).start()

    add_and_pass(1)
    drain(Gr3, grecv.at[2])
    total = Ib[x].astype(F32)
    for o in range(3):
        total += Gr3[o].astype(F32)
    Jb[z] = total.astype(BF16)
    for copy in g_z:
        copy.start()
    stage_two(0, 1)
    stage_two(0, 3)
    stage_two_own(0)
    stage_two(1, 2)
    drain(Jb.at[pl.ds(0, 3)], grecv.at[3])
    total = Jb[0].astype(F32)
    for o in range(1, 4):
        total += Jb[o].astype(F32)
    rows = pl.ds(pl.multiple_of(g * sub, sub), sub)
    Fin[g, 0] = (i1[rows] + total[0]).astype(BF16)
    Fin[g, 1] = total[1].astype(BF16)
    Fin[g, 2] = (i2[rows] + total[2]).astype(BF16)
    for copy in b_plane:
        copy.start()
    for dv in (1, 3):
        stage_two(1, dv)
    stage_two_own(1)
    stage_two_end(0)
    col = (-R[0]).astype(BF16)
    put(0, col)
    R[0] = jnp.dot(col, lk[...], preferred_element_type=F32) * m2[16 * r + c].astype(F32)
    drain(Fin.at[pl.ds(0, 15)], grecv.at[4])
    b_pair.start()
    stage_two_end(1)
    put(1, (-(R[1] + R[0])).astype(BF16))
    b_pair.wait_recv()
    d1 = Fin[:, 0].astype(F32).reshape(T, T).astype(BF16)
    s21 = Fin[:, 1].astype(F32).reshape(T, T)
    put(2, d1)
    cross = (s21.T - jnp.dot(d1, lk[...], preferred_element_type=F32)).astype(BF16)
    put(3, cross)
    d2 = Fin[:, 2].astype(F32).reshape(T, T)
    d2 = d2 - jnp.dot(s21.astype(BF16), lk[...], preferred_element_type=F32)
    turned = lax.dot_general(lk[...], cross, (((0,), (0,)), ((), ())), preferred_element_type=F32)
    put(4, (d2 - turned).astype(BF16))

    factors_left()
    drain(A.at[pl.ds(0, 3)], ssem.at[0])
    drain(A.at[0, pl.ds(0, 6)], ssem.at[1])
    g_pair.wait_send()
    drain(Gr2, gsend.at[1])
    drain(Gr3, gsend.at[2])
    drain(Jb.at[pl.ds(0, 3)], gsend.at[3])
    drain(Fin.at[pl.ds(0, 15)], gsend.at[4])
    b_pair.wait_send()
    drain(O, semO.at[0])


def hand_on(*refs):
    for k in range(5):
        refs[5 + k][...] = refs[k][...]


def shards(anc, tm, m1, m2, f1, f2, link, inv1, inv2):
    T = anc.shape[2]
    half, sub = T // 2, T // 32
    any_space = pl.BlockSpec(memory_space=pltpu.HBM)
    smem = pl.BlockSpec(memory_space=pltpu.SMEM)
    vmem = pl.BlockSpec(memory_space=pltpu.VMEM)
    dma = pltpu.SemaphoreType.DMA
    tile = jax.ShapeDtypeStruct((T, T), BF16)
    column = jax.ShapeDtypeStruct((1, T, T), BF16)
    parts = pl.pallas_call(
        kernel,
        out_shape=(column, column, tile, tile, tile),
        in_specs=[any_space, smem, smem, smem, any_space, any_space, any_space, any_space, any_space],
        out_specs=(any_space,) * 5,
        scratch_shapes=[
            pltpu.VMEM((5, T, T), BF16),
            dma((1,)),
            pltpu.VMEM((16, 8, T, T), BF16),
            pltpu.VMEM((2, 8, T, T), BF16),
            pltpu.VMEM((8, half, T), BF16),
            pltpu.VMEM((8, half, T), BF16),
            pltpu.VMEM((16, 2, T, T), BF16),
            pltpu.VMEM((8, T, T), F32),
            pltpu.VMEM((2, 16, T, T), BF16),
            pltpu.VMEM((2, 2, 2, 2, half, T), BF16),
            pltpu.VMEM((2, 2, 4, 2, half, T), BF16),
            pltpu.VMEM((2, 2, 3, half, T), BF16),
            pltpu.VMEM((2, T, T), F32),
            pltpu.VMEM((32, 3, sub, T), F32),
            pltpu.VMEM((32, 3, sub, T), BF16),
            pltpu.VMEM((16, 3, sub, T), BF16),
            pltpu.VMEM((16, 3, sub, T), BF16),
            pltpu.VMEM((3, 4, 3, sub, T), BF16),
            pltpu.VMEM((4, 3, sub, T), BF16),
            pltpu.VMEM((3, 3, sub, T), BF16),
            pltpu.VMEM((4, 3, sub, T), BF16),
            pltpu.VMEM((32, 3, sub, T), BF16),
            pltpu.VMEM((T, T), BF16),
            pltpu.VMEM((T, T), F32),
            pltpu.VMEM((T, T), F32),
            dma((2,)),
            dma((4,)),
            dma((2, 8)),
            dma((2,)),
            dma((5,)),
            dma((8,)),
            dma((1,)),
            dma((2,)),
            dma((2, 4)),
            dma((2, 2, 2)),
            dma((2, 2, 4)),
            dma((2, 2)),
            dma((6,)),
            dma((6,)),
        ],
        compiler_params=pltpu.CompilerParams(
            collective_id=0, has_side_effects=True, vmem_limit_bytes=60 * 1024 * 1024
        ),
    )(anc, tm.T, m1, m2, f1, f2, link, inv1, inv2)
    return pl.pallas_call(
        hand_on,
        out_shape=(column, column, tile, tile, tile),
        in_specs=[vmem] * 5,
        out_specs=(vmem,) * 5,
    )(*parts)


def solution(mesh):
    in_specs = (
        P("row", "col", None, None),
        P("row", "col"),
        P(),
        P(),
        P("row", None, None),
        P("row", None, None),
        P(),
        P(),
        P(),
    )
    out_specs = (P(("row", "col"), None, None), P(("row", "col"), None, None), P(), P(), P())
    return jax.shard_map(shards, mesh=mesh, in_specs=in_specs, out_specs=out_specs, check_vma=False)
```

```python
import jax
import jax.numpy as jnp
from jax import lax
from jax.experimental import pallas as pl
from jax.experimental.pallas import tpu as pltpu
from jax.sharding import PartitionSpec as P

MESH = pl.DeviceIdType.MESH
F32 = jnp.float32
BF16 = jnp.bfloat16
ORDER = (
    (2, 2), (2, 1), (1, 2), (2, 0), (0, 2), (2, 3), (3, 2), (1, 3),
    (3, 1), (1, 0), (0, 1), (1, 1), (3, 3), (3, 0), (0, 3), (0, 0),
)


def pick(index, values):
    out = jnp.int32(values[0])
    for k in range(1, len(values)):
        out = jnp.where(index == k, jnp.int32(values[k]), out)
    return out


def kernel(
    anc, tm_in, m1_in, m2_in, f1, f2, link, inv1, inv2,
    o1, o2, od1, oc, od2,
    O, semO, tm, m1, m2, A, L, X, Y, Fl, U, Pb, B1, B2, C, R, Gf, Gs, Gr1, Hb, Gr2, Ib, Gr3, Jb, Fin, lk, i1, i2,
    semA, semF, semLr, semLc, semLs, semXr, semY, ssem, rsem0, rsem1, rsem2, rsem3, gsend, grecv,
):
    T = anc.shape[2]
    half, sub = T // 2, T // 32
    r = lax.axis_index("row")
    c = lax.axis_index("col")
    y, core = r // 2, r % 2
    x, z = c // 4, c % 4

    def at(dx=0, dy=0, dz=0, other_core=None):
        which = core if other_core is None else other_core
        return {"row": ((y + dy) % 4) * 2 + which, "col": ((x + dx) % 4) * 4 + (z + dz) % 4}

    members = (m1, m2)

    def drain(ref, sem):
        pltpu.make_async_copy(ref, ref, sem).wait()


    d = (y + 4 - x) % 4
    own_core = core == z // 2
    off = 8 * (z % 2)
    is_src = jnp.logical_and(d == 0, own_core)
    inside = d != 0
    up_core = core == 0
    down_core = core == 1
    away = jnp.where(up_core, d, (4 - d) % 4)
    early = jnp.logical_or(away == 1, d == 0)

    def tile_of(k, up):
        return jnp.where(up, 0, 4) + k // 2

    def half_of(k):
        return pl.ds(k % 2 * half, half)

    def piece(p, k, up):
        return L.at[p, tile_of(k, up), half_of(k)]

    def stored(p, k, up):
        return (f1, f2)[p].at[off + tile_of(k, up), half_of(k)]

    def local_piece(p, k, up):
        return pltpu.make_async_copy(stored(p, k, up), piece(p, k, up), semLc.at[p])

    def along(p, k, up, src):
        return pltpu.make_async_remote_copy(
            src_ref=src, dst_ref=piece(p, k, up), send_sem=semLs.at[0], recv_sem=semLr.at[p, k],
            device_id=at(dy=jnp.where(up, 1, 3), other_core=jnp.where(up, 0, 1)), device_id_type=MESH,
        )

    def across(p, k, up):
        return pltpu.make_async_remote_copy(
            src_ref=piece(p, k, up), dst_ref=piece(p, k, up),
            send_sem=semLs.at[1], recv_sem=semLc.at[p],
            device_id=at(other_core=1 - core), device_id_type=MESH,
        )

    def detour_in(k, up):
        return pltpu.make_async_remote_copy(
            src_ref=Y.at[k], dst_ref=X.at[k], send_sem=semLs.at[2], recv_sem=semXr.at[k],
            device_id=at(dy=jnp.where(up, 3, 1), other_core=jnp.where(up, 0, 1)), device_id_type=MESH,
        )

    def detour_out(k):
        return pltpu.make_async_remote_copy(
            src_ref=X.at[k], dst_ref=piece(0, k, up_core), send_sem=semLs.at[3], recv_sem=semLr.at[0, k],
            device_id=at(dx=jnp.where(up_core, 1, 3)), device_id_type=MESH,
        )

    def straight(k, up):
        return pltpu.make_async_remote_copy(
            src_ref=piece(1, k, up), dst_ref=piece(1, k, up), send_sem=semLs.at[4], recv_sem=semLr.at[1, k],
            device_id=at(dy=jnp.where(up, 3, 1), other_core=jnp.where(up, 0, 1)), device_id_type=MESH,
        )

    lends = jnp.logical_and(own_core, jnp.logical_or(d == 1, d == 3))
    lends_up = d == 1

    def load_row(s):
        return pltpu.make_async_copy(anc.at[s], A.at[s], semA.at[s // 8])

    small = [
        pltpu.make_async_copy(f1, Fl.at[:, 0], semF.at[0]),
        pltpu.make_async_copy(f2, Fl.at[:, 1], semF.at[0]),
        pltpu.make_async_copy(link, lk, semF.at[1]),
        pltpu.make_async_copy(inv1, i1, semF.at[2]),
        pltpu.make_async_copy(inv2, i2, semF.at[3]),
        pltpu.make_async_copy(tm_in, tm, semF.at[4]),
        pltpu.make_async_copy(m1_in, m1, semF.at[5]),
        pltpu.make_async_copy(m2_in, m2, semF.at[6]),
    ]
    barrier = pltpu.get_barrier_semaphore()
    partners = [at(other_core=1 - core), at(dx=1), at(dx=3), at(dz=1), at(dz=3), at(dx=2), at(dy=2), at(dz=2)]
    for o in (1, 3):
        partners += [at(dy=o), at(dy=o, other_core=1 - core)]
    for partner in partners:
        pl.semaphore_signal(barrier, inc=1, device_id=partner, device_id_type=MESH)

    def lent(k):
        return pltpu.make_async_copy(stored(0, k, lends_up), Y.at[k], semY.at[0])

    @pl.when(lends)
    def _():
        @pl.loop(0, 8)
        def _(k):
            lent(k).start()

    for p in range(2):

        @pl.when(is_src)
        def _():
            @pl.loop(0, 8)
            def _(k):
                for up in (True, False):
                    local_piece(p, k, up).start()

        if p == 0:
            for copy in small:
                copy.start()

    for s in range(16):
        load_row(s).start()
    pl.semaphore_wait(barrier, len(partners))

    for p in range(2):

        @pl.when(is_src)
        def _():
            drain(A.at[0], semLc.at[p])

            @pl.loop(0, 8)
            def _(k):
                for up in (True, False):
                    along(p, k, up, piece(p, k, up)).start()

        if p == 0:

            @pl.when(lends)
            def _():
                drain(A.at[0, pl.ds(0, 4)], semY.at[0])

                @pl.loop(0, 8)
                def _(k):
                    detour_in(k, lends_up).start()

        if p == 1:

            @pl.when(is_src)
            def _():
                @pl.loop(0, 8)
                def _(k):
                    for up in (True, False):
                        straight(k, up).start()

    @pl.when(is_src)
    def _():
        for p in range(2):

            @pl.loop(0, 8)
            def _(k):
                for up in (True, False):
                    across(p, k, up).start()

    drain(Fl, semF.at[0])
    for copy in small[2:]:
        copy.wait()

    @pl.loop(0, 16)
    def _(s):
        two = jnp.full((T, T), m2[16 * r + s].astype(F32), F32).astype(BF16)
        Fl[s, 0] = Fl[s, 0].T
        Fl[s, 1] = (Fl[s, 1] * two).T

    def relay(p, k):
        @pl.when(inside)
        def _():
            along(p, k, up_core, piece(p, k, up_core)).wait_recv()

            @pl.when(away == 1)
            def _():
                along(p, k, up_core, piece(p, k, up_core)).start()

            across(p, k, up_core).start()

        if p == 0:

            @pl.when(d == 0)
            def _():
                detour_in(k, up_core).wait_recv()
                detour_out(k).start()

    def arrived(p):
        @pl.when(inside)
        def _():
            drain(A.at[0, pl.ds(0, 4)], semLc.at[p])

        @pl.when(jnp.logical_and(d == 0, jnp.logical_not(own_core)))
        def _():
            drain(A.at[0], semLc.at[p])

    def factors_left():
        @pl.when(is_src)
        def _():
            drain(A.at[pl.ds(0, 2)], semLs.at[0])
            drain(A.at[pl.ds(0, 2)], semLs.at[1])
            drain(A.at[0], semLs.at[4])

        @pl.when(away == 1)
        def _():
            drain(A.at[0], semLs.at[0])

        @pl.when(inside)
        def _():
            drain(A.at[0], semLs.at[1])

        @pl.when(lends)
        def _():
            drain(A.at[0, pl.ds(0, 4)], semLs.at[2])

        @pl.when(d == 0)
        def _():
            drain(A.at[0, pl.ds(0, 4)], semLs.at[3])

    def slot(h, du, dv):
        dx, dz = (du, dv) if h == 0 else (dv, du)
        return ((x + dx) % 4) * 4 + (z + dz) % 4

    def rs_copy(h, way, src, dst, sem):
        step = 1 if way == 0 else 3
        device = at(dx=step) if h == 0 else at(dz=step)
        return pltpu.make_async_remote_copy(
            src_ref=src, dst_ref=dst, send_sem=ssem.at[0], recv_sem=sem, device_id=device, device_id_type=MESH
        )

    def rows_of(h):
        return pl.ds(h * half, half)

    def first_hop(p, h, way, k, src):
        return rs_copy(h, way, src, B1.at[p, h, way, k], rsem1.at[p, h, way])

    def second_hop(p, h, way, dv, src):
        return rs_copy(h, way, src, B2.at[p, h, dv, way], rsem2.at[p, h, dv])

    def two_away(h, dv, src):
        device = at(dx=2) if h == 0 else at(dz=2)
        return pltpu.make_async_remote_copy(
            src_ref=src, dst_ref=B1.at[0, h, dv // 2, dv % 2],
            send_sem=ssem.at[0], recv_sem=rsem0.at[h, dv], device_id=device, device_id_type=MESH,
        )

    def third_hop(p, h, dv):
        device = at(dz=dv) if h == 0 else at(dx=dv)
        return pltpu.make_async_remote_copy(
            src_ref=B2.at[p, h, dv, 0], dst_ref=C.at[p, h, dv - 1],
            send_sem=ssem.at[1], recv_sem=rsem3.at[p, h], device_id=device, device_id_type=MESH,
        )

    def product(p, pair):
        places, weights = [], []
        for e in range(2):
            i = 2 * pair + e
            dx, dz = pick(i, [v[0] for v in ORDER]), pick(i, [v[1] for v in ORDER])
            s = ((x + dx) % 4) * 4 + (z + dz) % 4
            places.append((dx, dz, s))
            weights.append(members[p][16 * r + s])
        acc = None
        for j in range(8):
            other = members[p][8 * c + j]
            a = [masked(A[s, j], tm[j, s] * own * other) for (_, _, s), own in zip(places, weights)]
            term = jnp.dot(jnp.concatenate(a, 0), L[p, j], preferred_element_type=F32)
            acc = term if acc is None else acc + term
        for e, (dx, dz, s) in enumerate(places):
            Pb[p, s] = acc[e * T : (e + 1) * T].astype(BF16)
        for dx, dz, s in places:
            send_on(p, dx, dz, s)

    def masked(a, w):
        return a * jnp.full((T, T), w.astype(F32), F32).astype(BF16)

    def send_on(p, dx, dz, s):
        for h in range(2):
            du, dv = (dx, dz) if h == 0 else (dz, dx)
            inner = jnp.logical_or(dv == 1, dv == 2)
            outer = jnp.logical_not(inner)
            src = Pb.at[p, s, rows_of(h)]

            if p == 0:

                @pl.when(du == 1)
                def _():
                    second_hop(0, h, 0, dv, src).start()

                @pl.when(du == 3)
                def _():
                    second_hop(0, h, 1, dv, src).start()

                @pl.when(du == 2)
                def _():
                    two_away(h, dv, src).start()

                continue

            @pl.when(jnp.logical_and(du == 2, inner))
            def _():
                first_hop(p, h, 0, dv - 1, src).start()

            @pl.when(jnp.logical_and(du == 2, outer))
            def _():
                first_hop(p, h, 1, dv // 3, src).start()

            @pl.when(jnp.logical_and(du == 1, outer))
            def _():
                second_hop(p, h, 0, dv, src).start()

            @pl.when(jnp.logical_and(du == 3, inner))
            def _():
                second_hop(p, h, 1, dv, src).start()

    def add_and_pass(p):
        for h in range(2):
            for way in range(2):
                drain(B1.at[p, h, way], rsem1.at[p, h, way])
                for k in (1, 0):
                    du, dv = (1, k + 1) if way == 0 else (3, 3 * k)
                    mine = Pb[p, slot(h, du, dv), rows_of(h)].astype(F32)
                    B1[p, h, way, k] = (mine + B1[p, h, way, k].astype(F32)).astype(BF16)
                    second_hop(p, h, way, dv, B1.at[p, h, way, k]).start()

    def line_sum(p, h, dv):
        drain(B2.at[p, h, dv], rsem2.at[p, h, dv])
        total = Pb[p, slot(h, 0, dv), rows_of(h)].astype(F32)
        total += B2[p, h, dv, 0].astype(F32) + B2[p, h, dv, 1].astype(F32)
        if p == 0:
            drain(B1.at[0, h, dv // 2, dv % 2], rsem0.at[h, dv])
            total += B1[0, h, dv // 2, dv % 2].astype(F32)
        return total

    def stage_two_sum(p, dv):
        for h in range(2):
            B2[p, h, dv, 0] = line_sum(p, h, dv).astype(BF16)

    def stage_two(p, dv):
        stage_two_sum(p, dv)
        for h in range(2):
            third_hop(p, h, dv).start()

    def stage_two_own(p):
        for h in range(2):
            R[p, rows_of(h)] = line_sum(p, h, 0)

    def stage_two_end(p):
        for h in range(2):
            total = R[p, rows_of(h)]
            drain(C.at[p, h], rsem3.at[p, h])
            for dv in range(1, 4):
                total += C[p, h, dv - 1].astype(F32)
            R[p, rows_of(h)] = total

    def contract():
        @pl.loop(0, 4)
        def _(q):
            total = None
            for t in range(4):
                left = Fl[4 * q + t].reshape(2 * T, T)
                term = jnp.dot(left, Pb[0, 4 * q + t], preferred_element_type=F32)
                total = term if total is None else total + term
            pieces = [total[k * T : (k + 1) * T].reshape(32, sub, T) for k in range(2)]

            @pl.when(q == 0)
            def _():
                for k in range(2):
                    Gf[:, k] = pieces[k]

            @pl.when(q > 0)
            def _():
                for k in range(2):
                    Gf[:, k] += pieces[k]

    def from_left(t):
        q, j = t // 8, t % 8
        total = None
        for k in range(8):
            s = 8 * q + k
            term = jnp.dot(Fl[s, 1], masked(A[s, j], tm[j, s]), preferred_element_type=F32)
            total = term if total is None else total + term

        @pl.when(q == 0)
        def _():
            U[j] = total

        @pl.when(q > 0)
        def _():
            U[j] += total

    def finish_from_left():
        total = None
        for j in range(8):
            left = U[j].astype(BF16)
            term = jnp.dot(left, masked(L[1, j], m2[8 * c + j]), preferred_element_type=F32)
            total = term if total is None else total + term
        Gf[:, 2] = total.reshape(32, sub, T)

    @pl.loop(0, 16)
    def _(t):
        @pl.when(jnp.logical_and(early, jnp.logical_and(t >= 3, t < 11)))
        def _():
            relay(0, t - 3)

        @pl.when(jnp.logical_and(away == 1, jnp.logical_and(t >= 11, t < 15)))
        def _():
            relay(1, t - 11)

        @pl.when(jnp.logical_and(jnp.logical_not(early), t >= 8))
        def _():
            relay(0, t - 8)

        @pl.when(t % 8 == 0)
        def _():
            drain(A.at[pl.ds(0, 8)], semA.at[t // 8])

        from_left(t)

    arrived(0)

    @pl.loop(0, 8)
    def _(i):
        product(0, i)

        @pl.when(away == 2)
        def _():
            relay(1, i)

        @pl.when(jnp.logical_and(away == 3, i >= 4))
        def _():
            relay(1, i - 4)

        @pl.when(jnp.logical_and(away == 1, i < 4))
        def _():
            relay(1, 4 + i)

    contract()

    @pl.when(away == 3)
    def _():
        @pl.loop(4, 8)
        def _(k):
            relay(1, k)

    arrived(1)
    finish_from_left()
    Gs[...] = Gf[...].astype(BF16)

    def out_copy(k):
        return pltpu.make_async_copy(O.at[k], (o1.at[0], o2.at[0], od1, oc, od2)[k], semO.at[0])

    def put(k, value):
        O[k] = value
        out_copy(k).start()

    def g_copy(kind, src, dst, device):
        return pltpu.make_async_remote_copy(
            src_ref=src, dst_ref=dst, send_sem=gsend.at[kind], recv_sem=grecv.at[kind],
            device_id=device, device_id_type=MESH,
        )

    g = core * 16 + y * 4 + x
    plane = [(a, b) for a in range(4) for b in range(4) if (a, b) != (0, 0)]
    plane.sort(key=lambda v: -sum(min(e, 4 - e) for e in v))
    g_pair = g_copy(0, Gs.at[pl.ds((1 - core) * 16, 16)], Gr1, at(other_core=1 - core))
    b_pair = g_copy(5, Fin.at[pl.ds(core * 16, 16)], Fin.at[pl.ds(core * 16, 16)], at(other_core=1 - core))
    b_plane = []
    for a, b in plane:
        b_plane.append(g_copy(4, Fin.at[g], Fin.at[g], at(dx=a, dy=b)))
    g_y = [g_copy(1, Hb.at[pl.ds((y + o) % 4 * 4, 4)], Gr2.at[o - 1], at(dy=o)) for o in (2, 1, 3)]
    g_x = [g_copy(2, Ib.at[(x + o) % 4], Gr3.at[o - 1], at(dx=o)) for o in (2, 1, 3)]
    g_z = [g_copy(3, Jb.at[z], Jb.at[z], at(dz=o)) for o in (2, 1, 3)]

    g_pair.start()

    @pl.loop(0, 8)
    def _(i):
        product(1, i)

        @pl.when(i == 0)
        def _():
            g_pair.wait_recv()
            Hb[...] = (Gf[pl.ds(core * 16, 16)] + Gr1[...].astype(F32)).astype(BF16)
            for copy in g_y:
                copy.start()

        @pl.when(i == 6)
        def _():
            drain(Gr2, grecv.at[1])
            total = Hb[pl.ds(y * 4, 4)].astype(F32)
            for o in range(3):
                total += Gr2[o].astype(F32)
            Ib[...] = total.astype(BF16)
            stage_two_sum(0, 2)
            for copy in g_x:
                copy.start()
            for h in range(2):
                third_hop(0, h, 2).start()

    add_and_pass(1)
    drain(Gr3, grecv.at[2])
    total = Ib[x].astype(F32)
    for o in range(3):
        total += Gr3[o].astype(F32)
    Jb[z] = total.astype(BF16)
    for copy in g_z:
        copy.start()
    stage_two(0, 1)
    stage_two(0, 3)
    stage_two_own(0)
    stage_two(1, 2)
    drain(Jb.at[pl.ds(0, 3)], grecv.at[3])
    total = Jb[0].astype(F32)
    for o in range(1, 4):
        total += Jb[o].astype(F32)
    rows = pl.ds(pl.multiple_of(g * sub, sub), sub)
    Fin[g, 0] = (i1[rows] + total[0]).astype(BF16)
    Fin[g, 1] = total[1].astype(BF16)
    Fin[g, 2] = (i2[rows] + total[2]).astype(BF16)
    for copy in b_plane:
        copy.start()
    for dv in (1, 3):
        stage_two(1, dv)
    stage_two_own(1)
    stage_two_end(0)
    col = (-R[0]).astype(BF16)
    put(0, col)
    R[0] = jnp.dot(col, lk[...], preferred_element_type=F32) * m2[16 * r + c].astype(F32)
    drain(Fin.at[pl.ds(0, 15)], grecv.at[4])
    b_pair.start()
    stage_two_end(1)
    put(1, (-(R[1] + R[0])).astype(BF16))
    b_pair.wait_recv()
    d1 = Fin[:, 0].astype(F32).reshape(T, T).astype(BF16)
    s21 = Fin[:, 1].astype(F32).reshape(T, T)
    put(2, d1)
    cross = (s21.T - jnp.dot(d1, lk[...], preferred_element_type=F32)).astype(BF16)
    put(3, cross)
    d2 = Fin[:, 2].astype(F32).reshape(T, T)
    d2 = d2 - jnp.dot(s21.astype(BF16), lk[...], preferred_element_type=F32)
    turned = lax.dot_general(lk[...], cross, (((0,), (0,)), ((), ())), preferred_element_type=F32)
    put(4, (d2 - turned).astype(BF16))

    factors_left()
    drain(A.at[pl.ds(0, 3)], ssem.at[0])
    drain(A.at[0, pl.ds(0, 6)], ssem.at[1])
    g_pair.wait_send()
    drain(Gr2, gsend.at[1])
    drain(Gr3, gsend.at[2])
    drain(Jb.at[pl.ds(0, 3)], gsend.at[3])
    drain(Fin.at[pl.ds(0, 15)], gsend.at[4])
    b_pair.wait_send()
    drain(O, semO.at[0])


def hand_on(*refs):
    for k in range(5):
        refs[5 + k][...] = refs[k][...]


def shards(anc, tm, m1, m2, f1, f2, link, inv1, inv2):
    T = anc.shape[2]
    half, sub = T // 2, T // 32
    any_space = pl.BlockSpec(memory_space=pltpu.HBM)
    vmem = pl.BlockSpec(memory_space=pltpu.VMEM)
    dma = pltpu.SemaphoreType.DMA
    tile = jax.ShapeDtypeStruct((T, T), BF16)
    column = jax.ShapeDtypeStruct((1, T, T), BF16)
    parts = pl.pallas_call(
        kernel,
        out_shape=(column, column, tile, tile, tile),
        in_specs=[any_space, any_space, any_space, any_space, any_space, any_space, any_space, any_space, any_space],
        out_specs=(any_space,) * 5,
        scratch_shapes=[
            pltpu.VMEM((5, T, T), BF16),
            dma((1,)),
            pltpu.SMEM(tm.shape[::-1], jnp.int32),
            pltpu.SMEM(m1.shape, jnp.int32),
            pltpu.SMEM(m2.shape, jnp.int32),
            pltpu.VMEM((16, 8, T, T), BF16),
            pltpu.VMEM((2, 8, T, T), BF16),
            pltpu.VMEM((8, half, T), BF16),
            pltpu.VMEM((8, half, T), BF16),
            pltpu.VMEM((16, 2, T, T), BF16),
            pltpu.VMEM((8, T, T), F32),
            pltpu.VMEM((2, 16, T, T), BF16),
            pltpu.VMEM((2, 2, 2, 2, half, T), BF16),
            pltpu.VMEM((2, 2, 4, 2, half, T), BF16),
            pltpu.VMEM((2, 2, 3, half, T), BF16),
            pltpu.VMEM((2, T, T), F32),
            pltpu.VMEM((32, 3, sub, T), F32),
            pltpu.VMEM((32, 3, sub, T), BF16),
            pltpu.VMEM((16, 3, sub, T), BF16),
            pltpu.VMEM((16, 3, sub, T), BF16),
            pltpu.VMEM((3, 4, 3, sub, T), BF16),
            pltpu.VMEM((4, 3, sub, T), BF16),
            pltpu.VMEM((3, 3, sub, T), BF16),
            pltpu.VMEM((4, 3, sub, T), BF16),
            pltpu.VMEM((32, 3, sub, T), BF16),
            pltpu.VMEM((T, T), BF16),
            pltpu.VMEM((T, T), F32),
            pltpu.VMEM((T, T), F32),
            dma((2,)),
            dma((7,)),
            dma((2, 8)),
            dma((2,)),
            dma((5,)),
            dma((8,)),
            dma((1,)),
            dma((2,)),
            dma((2, 4)),
            dma((2, 2, 2)),
            dma((2, 2, 4)),
            dma((2, 2)),
            dma((6,)),
            dma((6,)),
        ],
        compiler_params=pltpu.CompilerParams(
            collective_id=0, has_side_effects=True, vmem_limit_bytes=60 * 1024 * 1024
        ),
    )(anc, tm.T, m1, m2, f1, f2, link, inv1, inv2)
    return pl.pallas_call(
        hand_on,
        out_shape=(column, column, tile, tile, tile),
        in_specs=[vmem] * 5,
        out_specs=(vmem,) * 5,
    )(*parts)


def solution(mesh):
    in_specs = (
        P("row", "col", None, None),
        P("row", "col"),
        P(),
        P(),
        P("row", None, None),
        P("row", None, None),
        P(),
        P(),
        P(),
    )
    out_specs = (P(("row", "col"), None, None), P(("row", "col"), None, None), P(), P(), P())
    return jax.shard_map(shards, mesh=mesh, in_specs=in_specs, out_specs=out_specs, check_vma=False)
```
